128 devices in a mesh: row: 8 (over z_lo, x), col: 16 (over z_hi, y, core).
Axes of the slice: x: 4, y: 4, z: 4 (z_hi: 2, z_lo: 2; z = z_hi * 2 + z_lo), core: 2. Of those that a mesh axis runs over, the one named last changes fastest.
Arguments:
- grad: float32 [7168, 8192], P(('row', 'col')), may hold values from -60 to 60
- momentum: float32 [7168, 8192], P(('row', 'col')), may hold values from -6 to 6
Outputs:
- update: bfloat16 [7168, 8192], P(('row', 'col'))
- new_momentum: float32 [7168, 8192], P(('row', 'col'))
The draws below stay inside these ranges and needn't reach their ends.
All inputs are finite; a program needn't handle non-finite values.
Results may differ from the reference program's by a relative error of at most 0.02.
Values may be sent and summed in bfloat16 or wider, within the bound.
A program may use at most 128 MiB of HBM per device.

```python
import math
import jax
import jax.numpy as jnp
from jax import lax

M = 7168
N = 8192
NB = 512


def draw_grad(key, part):
    keys = jax.random.split(key, 3)
    base_vals = jnp.clip(jax.random.normal(keys[0], (M, N), jnp.float32), -4.0, 4.0)
    row_scale = jnp.exp(jax.random.uniform(keys[1], (M, 1), jnp.float32, 0.0, math.log(10.0)))
    col_scale = jnp.exp(jax.random.uniform(keys[2], (1, N), jnp.float32, 0.0, math.log(10.0)))
    trend = jnp.exp(math.log(3.0) * jnp.arange(M, dtype=jnp.float32) / M).reshape(M, 1)
    return (0.05 * base_vals * row_scale * col_scale * trend).astype(jnp.float32)


def level_of(stream_key, extent, cuts, low, largest):
    gain, own = 1.0, jax.random.fold_in(stream_key, 6)
    for dim, blocks in cuts:
        steps = jnp.exp(jax.random.uniform(jax.random.fold_in(own, dim), (blocks,), jnp.float32, low / len(cuts), largest / len(cuts)))
        gain = gain * jnp.repeat(steps, extent[dim] // blocks).reshape([-1 if axis == dim else 1 for axis in range(len(extent))])
    return gain


def gaussian(own_key, dims, width, reach, cuts=(), held_as=jnp.bfloat16):
    level = level_of(own_key, dims, cuts, -0.22, 0.18) if cuts else 1.0
    array = jax.random.normal(own_key, dims, jnp.float32) * width * level
    return jnp.minimum(jnp.maximum(array, -reach), reach).astype(held_as)


def setup_inputs(seed: int = 0) -> dict:
    arg_keys = jax.random.split(jax.random.key(seed), 3)
    return {
        "grad": draw_grad(jax.random.fold_in(arg_keys[2], 71), 0),
        "momentum": gaussian(arg_keys[1], (M, N), 1.0, 6.0, ((0, 128),), jnp.float32),
    }


momentum_coef = 0.95
rms_target = 0.4
coef_a = 3.4445
coef_b = -4.775
coef_c = 2.0315

def reference(grad, momentum):
    new_momentum = momentum_coef * momentum + grad
    direction = grad + momentum_coef * new_momentum
    sumsq = jnp.sum(direction * direction)
    factor = rms_target * jnp.sqrt(jnp.float32(M)) / (jnp.sqrt(sumsq) + 1e-07)
    start = (direction * factor).astype(jnp.bfloat16)
    start_wide = start.astype(jnp.float32)
    groups = start_wide.reshape(M, N // NB, NB).transpose(1, 0, 2)

    def add_group(carry, group):
        partial_gram = jnp.dot(group, group.T, precision=lax.Precision.HIGHEST)
        rounded = lax.optimization_barrier(partial_gram.astype(jnp.bfloat16))
        return (carry + rounded.astype(jnp.float32), None)
    summed, unused = lax.scan(add_group, jnp.zeros((M, M), jnp.float32), groups)
    gram = lax.optimization_barrier(summed.astype(jnp.bfloat16)).astype(jnp.float32)
    first = jnp.dot(gram, start_wide, precision=lax.Precision.HIGHEST)
    first_round = lax.optimization_barrier(first.astype(jnp.bfloat16)).astype(jnp.float32)
    second = jnp.dot(gram, first_round, precision=lax.Precision.HIGHEST)
    scale_out = 0.2 * jnp.sqrt(jnp.float32(max(M, N)))
    result = coef_a * start_wide + coef_b * first + coef_c * second
    return ((result * scale_out).astype(jnp.bfloat16), new_momentum)
```

```python
import math

import jax
import jax.numpy as jnp
from jax import lax
from jax.experimental import pallas as pl
from jax.experimental.pallas import tpu as pltpu
from jax.sharding import PartitionSpec as P

M = 7168
N = 8192

momentum_coef = 0.95
rms_target = 0.4
coef_a = 3.4445
coef_b = -4.775
coef_c = 2.0315
scale_out = 0.2 * math.sqrt(max(M, N))

BF = jnp.bfloat16
F32 = jnp.float32
MESH = pl.DeviceIdType.MESH

RING = 4
ROWS = 56
UNIT = RING * ROWS
KB = N // RING
AR = RING * UNIT
BR = 2 * AR
T = 4
TR = AR // T
QR = TR // RING
NT = 8
NW = KB // NT
GH = BR // 2
FH = KB // 2
UH = UNIT // 2
N_SEM = 256


def kernel(d_ref, ss_ref, out_ref, a_ref, b_ref, gp, g1buf, g2buf, gf, gt, fp, f1buf, f2buf, hf, sp, sr, s1buf, s2buf,
           ub, orx, ssb, sst, send, recv, lsem):
    row = lax.axis_index("row")
    col = lax.axis_index("col")
    x = row % 4
    h = col % 2
    y = (col // 2) % 4
    z = (col // 8) * 2 + row // 4

    def dev(dx=0, dy=0, dz=0, dh=0):
        nx, ny, nz, nh = (x + dx) % 4, (y + dy) % 4, (z + dz) % 4, (h + dh) % 2
        return {"row": (nz % 2) * 4 + nx, "col": (nz // 2) * 8 + ny * 2 + nh}

    zd = {k: dev(dz=k) for k in (1, 2, 3)}
    yd = {k: dev(dy=k) for k in (1, 2, 3)}
    xd = {k: dev(dx=k) for k in (1, 2, 3)}
    partner = dev(dh=1)

    barrier = pltpu.get_barrier_semaphore()
    peers = [partner] + [r[k] for r in (zd, yd, xd) for k in (1, 2, 3)]
    for p in peers:
        pl.semaphore_signal(barrier, inc=1, device_id=p, device_id_type=MESH)
    pl.semaphore_wait(barrier, len(peers))

    started = []

    def rc(src, dst, device):
        i = len(started)
        c = pltpu.make_async_remote_copy(
            src_ref=src, dst_ref=dst, send_sem=send.at[i], recv_sem=recv.at[i], device_id=device, device_id_type=MESH)
        c.start()
        started.append(c)
        return c

    def al(v, m=8):
        return pl.multiple_of(v, m)

    def ss_send(stage, devices):
        return [rc(sst.at[stage], ssb.at[stage, i], d) for i, d in enumerate(devices)]

    def ss_recv(stage, copies):
        tot = sst[stage]
        for i, c in enumerate(copies):
            c.wait_recv()
            tot = tot + ssb[stage, i]
        sst[stage + 1] = tot

    sst[0] = ss_ref[...]
    ssc = ss_send(0, [partner])

    def unit_rows(i):
        return pl.ds(al(i * UNIT), UNIT)

    own_slot = pl.ds(al(y * UNIT + z * ROWS), ROWS)
    a2a = []
    for k in (1, 3, 2):
        a2a.append(rc(d_ref.at[:, pl.ds(al(((z + k) % 4) * KB, 128), KB)], a_ref.at[own_slot, :], zd[k]))
    lc = pltpu.make_async_copy(d_ref.at[:, pl.ds(al(z * KB, 128), KB)], a_ref.at[own_slot, :], lsem.at[0])
    lc.start()
    ss_recv(0, ssc)
    ssc = ss_send(1, [zd[1], zd[3], zd[2]])
    lc.wait()
    for c in a2a:
        c.wait_recv()
    ss_recv(1, ssc)
    ssc = ss_send(2, [yd[1], yd[3], yd[2]])

    halves = (pl.ds(0, FH), pl.ds(FH, FH))
    own_a = unit_rows(y)
    ub_i = h * 4 + x

    def bu(k):
        return unit_rows(h * 4 + (x + k) % 4)

    def au(k):
        return unit_rows((y + k) % 4)

    own_b = unit_rows(ub_i)
    ya = {}
    xa = {}
    for first in (True, False):
        hr, hl = (0, 1) if first else (1, 0)
        ya["R", hr] = rc(a_ref.at[own_a, halves[hr]], a_ref.at[own_a, halves[hr]], yd[1])
        ya["L", hl] = rc(a_ref.at[own_a, halves[hl]], a_ref.at[own_a, halves[hl]], yd[3])
        xa["R", hr] = rc(a_ref.at[own_a, halves[hr]], b_ref.at[own_b, halves[hr]], xd[1])
        xa["L", hl] = rc(a_ref.at[own_a, halves[hl]], b_ref.at[own_b, halves[hl]], xd[3])
    core = [rc(a_ref.at[own_a, :], b_ref.at[own_b, :], partner)]
    lb = pltpu.make_async_copy(a_ref.at[own_a, :], b_ref.at[own_b, :], lsem.at[1])
    lb.start()
    ss_recv(2, ssc)
    ssc = ss_send(3, [xd[1], xd[3], xd[2]])
    yf = []
    xf = []
    ya["R", 0].wait_recv()
    yf.append(rc(a_ref.at[au(3), halves[0]], a_ref.at[au(3), halves[0]], yd[1]))
    xa["R", 0].wait_recv()
    xf.append(rc(b_ref.at[bu(3), halves[0]], b_ref.at[bu(3), halves[0]], xd[1]))
    ya["L", 1].wait_recv()
    yf.append(rc(a_ref.at[au(1), halves[1]], a_ref.at[au(1), halves[1]], yd[3]))
    xa["L", 1].wait_recv()
    xf.append(rc(b_ref.at[bu(1), halves[1]], b_ref.at[bu(1), halves[1]], xd[3]))
    ss_recv(3, ssc)
    xa["R", 1].wait_recv()
    core.append(rc(b_ref.at[bu(3), :], b_ref.at[bu(3), :], partner))
    xa["L", 0].wait_recv()
    core.append(rc(b_ref.at[bu(1), :], b_ref.at[bu(1), :], partner))
    for c in xf:
        c.wait_recv()
    core.append(rc(b_ref.at[bu(2), :], b_ref.at[bu(2), :], partner))
    ya["R", 1].wait_recv()
    ya["L", 0].wait_recv()
    for c in yf:
        c.wait_recv()
    lb.wait()
    for c in core:
        c.wait_recv()

    factor = rms_target * math.sqrt(M) / (jnp.sqrt(sst[4][0:1, 0:1]) + 1e-07)
    factor2 = factor * factor

    class Ring:
        def __init__(self, pos, rd, part, r1, r2, full):
            self.p, self.rd, self.part, self.r1, self.r2, self.full = pos, rd, part, r1, r2, full

        def q(self, k):
            return (self.p + k) % 4

        def rs1(self):
            part, rd = self.part, self.rd
            self.c_a = rc(part(self.q(2), 0), self.r1(0), rd[1])
            self.c_b = rc(part(self.q(2), 1), self.r1(1), rd[3])
            self.c = [rc(part(self.q(1), 1), self.r2(0, 1), rd[1]), rc(part(self.q(3), 0), self.r2(1, 0), rd[3])]

        def rs2(self):
            part, rd = self.part, self.rd
            for c, k, hh, side in ((self.c_a, 1, 0, 0), (self.c_b, 3, 1, 1)):
                c.wait_recv()
                ref = part(self.q(k), hh)
                ref[...] = (ref[...].astype(F32) + self.r1(hh)[...].astype(F32)).astype(BF)
                self.c.append(rc(ref, self.r2(side, hh), rd[k]))

        def rs3(self, finish):
            for c in self.c:
                c.wait_recv()
            for hh in (0, 1):
                tot = (self.part(self.p, hh)[...].astype(F32) + self.r2(0, hh)[...].astype(F32)
                       + self.r2(1, hh)[...].astype(F32))
                finish(hh, tot)

        def ag1(self):
            full, rd, p = self.full, self.rd, self.p
            self.a_r0 = rc(full(p, 0), full(p, 0), rd[1])
            self.a_l1 = rc(full(p, 1), full(p, 1), rd[3])
            self.rest = [rc(full(p, 1), full(p, 1), rd[1]), rc(full(p, 0), full(p, 0), rd[3])]

        def ag2(self):
            full, rd = self.full, self.rd
            self.a_r0.wait_recv()
            self.rest.append(rc(full(self.q(3), 0), full(self.q(3), 0), rd[1]))
            self.a_l1.wait_recv()
            self.rest.append(rc(full(self.q(1), 1), full(self.q(1), 1), rd[3]))

        def ag3(self):
            for c in self.rest:
                c.wait_recv()

    def g_ring(t):
        def sl(buf):
            return lambda q, hh: buf.at[pl.ds(al(t * TR + q * QR), QR), pl.ds(hh * GH, GH)]
        return Ring(z, zd, sl(gp), lambda hh: g1buf.at[t, hh], lambda s, hh: g2buf.at[t, s, hh], sl(gf))

    def f_ring(t):
        def sl(buf):
            return lambda q, hh: buf.at[pl.ds(al(t * TR + q * QR), QR), pl.ds(hh * FH, FH)]
        return Ring(y, yd, sl(fp), lambda hh: f1buf.at[t, hh], lambda s, hh: f2buf.at[t, s, hh], sl(hf))

    gr = [g_ring(t) for t in range(T)]
    fr = [f_ring(t) for t in range(T)]

    def g0(t):
        rows = pl.ds(t * TR, TR)

        def body(j, carry):
            js = pl.ds(al(j * 256, 256), 256)
            gp[rows, js] = lax.dot_general(
                a_ref[rows, :], b_ref[js, :], (((1,), (1,)), ((), ())), preferred_element_type=F32).astype(BF)
            return carry

        lax.fori_loop(0, BR // 256, body, 0)
        gr[t].rs1()

    def g1(t):
        gr[t].rs2()

    def g2(t):
        def finish(hh, tot):
            gr[t].full(z, hh)[...] = (tot * jnp.broadcast_to(factor2, tot.shape)).astype(BF)
        gr[t].rs3(finish)
        gr[t].ag1()

    def g3(t):
        gr[t].ag2()

    def f0(t):
        gr[t].ag3()
        rows = pl.ds(t * TR, TR)

        def body(j, carry):
            js = pl.ds(al(j * 256, 256), 256)
            fp[rows, js] = jnp.dot(gf[rows, :], b_ref[:, js], preferred_element_type=F32).astype(BF)
            return carry

        lax.fori_loop(0, KB // 256, body, 0)
        fr[t].rs1()

    def f1(t):
        fr[t].rs2()

    def f2(t):
        def finish(hh, tot):
            d = a_ref[pl.ds(al(t * TR + y * QR), QR), pl.ds(hh * FH, FH)].astype(F32)
            fr[t].full(y, hh)[...] = (coef_b * d + coef_c * tot).astype(BF)
        fr[t].rs3(finish)
        fr[t].ag1()

    def f3(t):
        fr[t].ag2()

    def f4(t):
        fr[t].ag3()

    def transpose(c):
        rows = pl.ds(c * 128, 128)
        gt[:, rows] = gf[rows, :].T

    def step(fn, t):
        if 0 <= t < T:
            fn(t)

    for s in range(T + 4):
        step(g0, s)
        step(g2, s - 1)
        step(g1, s)
        step(f0, s - 2)
        step(g3, s - 1)
        step(f2, s - 3)
        step(f1, s - 2)
        step(f4, s - 4)
        step(f3, s - 3)
        if s == T + 1:
            for c in range(AR // 128):
                transpose(c)

    def s_ring(n):
        def part(q, hh):
            return sp.at[n, h, q, pl.ds(hh * UH, UH), :]
        return Ring(x, xd, part, lambda hh: s1buf.at[n, hh], lambda s, hh: s2buf.at[n, s, hh], None)

    srr = [s_ring(n) for n in range(NT)]
    ex = [None] * NT
    back = []

    def s_mm(n, hb):
        ns = pl.ds(n * NW, NW)

        def body(i, carry):
            r = pl.ds(al(hb * AR + i * UNIT), UNIT)
            sp[n, hb, i] = jnp.dot(gt[r, :], hf[:, ns], preferred_element_type=F32).astype(BF)
            return carry

        lax.fori_loop(0, RING, body, 0)

    def s0(n):
        s_mm(n, 1 - h)
        ex[n] = rc(sp.at[n, 1 - h], sr.at[n], partner)
        s_mm(n, h)

    def s1(n):
        ex[n].wait_recv()

        def body(i, carry):
            sp[n, h, i] = (sp[n, h, i].astype(F32) + sr[n, i].astype(F32)).astype(BF)
            return carry

        lax.fori_loop(0, RING, body, 0)
        srr[n].rs1()

    def s2(n):
        srr[n].rs2()

    def s3(n):
        ns = pl.ds(n * NW, NW)

        def finish(hh, tot):
            d = a_ref[pl.ds(al(y * UNIT + hh * UH), UH), ns].astype(F32)
            u = (coef_a * d + tot) * jnp.broadcast_to(factor * scale_out, tot.shape)
            ub[pl.ds(hh * UH, UH), ns] = u.astype(BF)

        srr[n].rs3(finish)
        for k in (1, 3, 2):
            back.append(rc(ub.at[pl.ds(al(((z + k) % 4) * ROWS), ROWS), ns], orx.at[z, :, ns], zd[k]))

    for s in range(NT + 3):
        for fn, lag in ((s0, 0), (s1, 1), (s2, 2), (s3, 3)):
            if 0 <= s - lag < NT:
                fn(s - lag)

    orx[z] = ub[pl.ds(al(z * ROWS), ROWS), :]
    for c in back:
        c.wait_recv()
    for i in range(RING):
        out_ref[:, pl.ds(i * KB, KB)] = orx[i]
    for c in started:
        c.wait_send()


def muon(d, ss):
    def v(*shape):
        return pltpu.VMEM(shape, BF)

    vm = pl.BlockSpec(memory_space=pltpu.VMEM)
    return pl.pallas_call(
        kernel,
        out_shape=jax.ShapeDtypeStruct((ROWS, N), BF),
        in_specs=[vm, vm],
        out_specs=vm,
        scratch_shapes=[
            v(AR, KB), v(BR, KB),
            v(AR, BR), v(T, 2, QR, GH), v(T, 2, 2, QR, GH), v(AR, BR), v(BR, AR),
            v(AR, KB), v(T, 2, QR, FH), v(T, 2, 2, QR, FH), v(AR, KB),
            v(NT, 2, RING, UNIT, NW), v(NT, RING, UNIT, NW), v(NT, 2, UH, NW), v(NT, 2, 2, UH, NW),
            v(UNIT, KB), v(RING, ROWS, KB),
            pltpu.VMEM((4, 3, 8, 128), F32), pltpu.VMEM((5, 8, 128), F32),
            pltpu.SemaphoreType.DMA((N_SEM,)), pltpu.SemaphoreType.DMA((N_SEM,)), pltpu.SemaphoreType.DMA((2,)),
        ],
        compiler_params=pltpu.CompilerParams(collective_id=0, has_side_effects=True, vmem_limit_bytes=63 << 20),
    )(d, ss)


def shards(grad, momentum):
    new_momentum = momentum_coef * momentum + grad
    direction = grad + momentum_coef * new_momentum
    ss = jnp.broadcast_to(jnp.sum(direction * direction), (8, 128))
    return muon(direction.astype(BF), ss), new_momentum


def solution(mesh):
    return jax.shard_map(
        shards,
        mesh=mesh,
        in_specs=(P(("row", "col"), None), P(("row", "col"), None)),
        out_specs=(P(("row", "col"), None), P(("row", "col"), None)),
        check_vma=False,
    )
```

```python
import math

import jax
import jax.numpy as jnp
from jax import lax
from jax.experimental import pallas as pl
from jax.experimental.pallas import tpu as pltpu
from jax.sharding import PartitionSpec as P

M = 7168
N = 8192

momentum_coef = 0.95
rms_target = 0.4
coef_a = 3.4445
coef_b = -4.775
coef_c = 2.0315
scale_out = 0.2 * math.sqrt(max(M, N))

BF = jnp.bfloat16
F32 = jnp.float32
MESH = pl.DeviceIdType.MESH

RING = 4
ROWS = 56
UNIT = RING * ROWS
KB = N // RING
AR = RING * UNIT
BR = 2 * AR
T = 7
TR = AR // T
QR = TR // RING
NT = 8
NW = KB // NT
GH = BR // 2
FH = KB // 2
UH = UNIT // 2
N_SEM = 400
WINDOW_G = 2
WINDOW_F = 3
WINDOW_S = 3

LINK_US = 1e6 / 44.5e9
CORE_US = 1e6 / 250e9
HOP_US = 1.7
SHOW = None


class Task:
    def __init__(self, name, cost, prio, fn=None, waits=(), sends=(), deps=()):
        self.name, self.cost, self.prio, self.fn = name, cost, prio, fn
        self.waits, self.sends, self.deps = list(waits), list(sends), list(deps)


def order_of(tasks):
    now, free, arrive, done, order = 0.0, {}, {}, set(), []
    todo = list(tasks)
    while todo:
        best = None
        for i, k in enumerate(todo):
            if any(d not in done for d in k.deps) or any(w not in arrive for w in k.waits):
                continue
            ready = max([arrive[w] for w in k.waits], default=0.0)
            key = (max(ready, now), k.prio, i)
            if best is None or key < best[0]:
                best = (key, k)
        key, k = best
        todo.remove(k)
        now = key[0] + k.cost
        for name, link, us, _ in k.sends:
            fin = max(now, free.get(link, 0.0)) + us
            free[link] = fin
            arrive[name] = fin + HOP_US
        done.add(k.name)
        order.append((k, key[0], now))
    return order


def kernel(grad_ref, mom_ref, out_ref, nm_ref, gin, minb, dbuf, a_ref, b_ref, gp, g1buf, g2buf, gf, gt, fp, f1buf, f2buf, hf,
           sp, sr, s1buf, s2buf, ub, ssb, sst, send, recv, lsem):
    row = lax.axis_index("row")
    col = lax.axis_index("col")
    x = row % 4
    h = col % 2
    y = (col // 2) % 4
    z = (col // 8) * 2 + row // 4

    def dev(dx=0, dy=0, dz=0, dh=0):
        nx, ny, nz, nh = (x + dx) % 4, (y + dy) % 4, (z + dz) % 4, (h + dh) % 2
        return {"row": (nz % 2) * 4 + nx, "col": (nz // 2) * 8 + ny * 2 + nh}

    zd = {k: dev(dz=k) for k in (1, 2, 3)}
    yd = {k: dev(dy=k) for k in (1, 2, 3)}
    xd = {k: dev(dx=k) for k in (1, 2, 3)}
    partner = dev(dh=1)

    def al(v, m=8):
        return pl.multiple_of(v, m)

    def cols(k):
        return pl.ds(al(((z + k) % 4) * KB, 128), KB)

    loads = {}
    for k in (0, 1, 3, 2):
        loads[k] = [pltpu.make_async_copy(grad_ref.at[:, cols(k)], gin.at[k], lsem.at[2 * k]),
                    pltpu.make_async_copy(mom_ref.at[:, cols(k)], minb.at[k], lsem.at[2 * k + 1])]
        for c in loads[k]:
            c.start()

    barrier = pltpu.get_barrier_semaphore()
    peers = [partner] + [r[k] for r in (zd, yd, xd) for k in (1, 2, 3)]
    for p in peers:
        pl.semaphore_signal(barrier, inc=1, device_id=p, device_id_type=MESH)

    copies = {}
    waited = set()

    def issue(name, src, dst, device):
        i = len(copies)
        c = pltpu.make_async_remote_copy(
            src_ref=src, dst_ref=dst, send_sem=send.at[i], recv_sem=recv.at[i], device_id=device, device_id_type=MESH)
        c.start()
        copies[name] = c

    tasks = []

    def add(*args, **kw):
        tasks.append(Task(*args, **kw))

    def us(rows, columns):
        return rows * columns * 2 * LINK_US

    def unit_rows(i):
        return pl.ds(al(i * UNIT), UNIT)

    def piece(unit, k):
        return pl.ds(al(unit * UNIT + ((z + k) % 4) * ROWS), ROWS)

    stores = []

    def pre(k):
        for c in loads[k]:
            c.wait()
        g = gin[k]
        nm = momentum_coef * minb[k] + g
        d = g + momentum_coef * nm
        minb[k] = nm
        c = pltpu.make_async_copy(minb.at[k], nm_ref.at[:, cols(k)], lsem.at[8 + k])
        c.start()
        stores.append(c)
        if k == 0:
            a_ref[piece(y, 0), :] = d.astype(BF)
        else:
            dbuf[k] = d.astype(BF)
        s = jnp.sum(jnp.sum(d * d, axis=0, keepdims=True), axis=1, keepdims=True)
        s = jnp.broadcast_to(s, (8, 128))
        sst[0] = s if k == 0 else sst[0] + s

    pre(0)
    pl.semaphore_wait(barrier, len(peers))

    halves = (pl.ds(0, FH), pl.ds(FH, FH))

    def bunit(k):
        return h * 4 + (x + k) % 4

    def aunit(k):
        return (y + k) % 4

    lbs = []

    def ag_sends(k):
        pa, pb = piece(y, k), piece(h * 4 + x, k)
        w = us(ROWS, FH)
        out = []
        for hr, hl in ((0, 1), (1, 0)):
            for ax, rd, ref, rows in (("y", yd, a_ref, pa), ("x", xd, b_ref, pb)):
                out.append((f"{ax}R{hr}{k}", ax + "+", w, lambda hh=hr, rd=rd, ref=ref, rows=rows: (
                    a_ref.at[pa, halves[hh]], ref.at[rows, halves[hh]], rd[1])))
                out.append((f"{ax}L{hl}{k}", ax + "-", w, lambda hh=hl, rd=rd, ref=ref, rows=rows: (
                    a_ref.at[pa, halves[hh]], ref.at[rows, halves[hh]], rd[3])))
        out.append((f"c0{k}", "c", ROWS * KB * 2 * CORE_US, lambda: (a_ref.at[pa, :], b_ref.at[pb, :], partner)))
        return out

    def local_b(k):
        c = pltpu.make_async_copy(a_ref.at[piece(y, k), :], b_ref.at[piece(h * 4 + x, k), :], lsem.at[12 + k])
        c.start()
        lbs.append(c)

    def cp(ref, rows, hh, device):
        return lambda: (ref.at[rows, hh], ref.at[rows, hh], device)

    add("ag0", 0.1, 0, lambda: local_b(0), sends=ag_sends(0))
    for k in (1, 3, 2):
        add(f"pre{k}", 0.5, 1, lambda k=k: pre(k), sends=[
            (f"z{k}", "z-" if k == 3 else "z+", us(ROWS, KB) * (2 if k == 2 else 1),
             lambda k=k: (dbuf.at[k], a_ref.at[piece(y, 0), :], zd[k]))])
    for k, src in ((3, 1), (1, 3), (2, 2)):
        add(f"ag{k}", 0.1, 0, lambda k=k: local_b(k), waits=[f"z{src}"], sends=ag_sends(k))
    for k in (0, 3, 1, 2):
        w = us(ROWS, FH)
        for ax, rd, ref, un in (("y", yd, a_ref, aunit), ("x", xd, b_ref, bunit)):
            add(f"{ax}fR{k}", 0.05, 0, waits=[f"{ax}R0{k}"], sends=[
                (f"{ax}FR{k}", ax + "+", w, lambda k=k, rd=rd, ref=ref, un=un: cp(ref, piece(un(3), k), halves[0], rd[1])())])
            add(f"{ax}fL{k}", 0.05, 0, waits=[f"{ax}L1{k}"], sends=[
                (f"{ax}FL{k}", ax + "-", w, lambda k=k, rd=rd, ref=ref, un=un: cp(ref, piece(un(1), k), halves[1], rd[3])())])
        for j, ws, ds in ((3, [f"xR1{k}"], [f"xfR{k}"]), (1, [f"xL0{k}"], [f"xfL{k}"]), (2, [f"xFR{k}", f"xFL{k}"], [])):
            add(f"core{j}{k}", 0.05, 1, waits=ws, deps=ds, sends=[
                (f"c{j}{k}", "c", ROWS * KB * 2 * CORE_US,
                 lambda j=j, k=k: cp(b_ref, piece(bunit(j), k), pl.ds(0, KB), partner)())])

    stages = [("c", [partner]), ("z", [zd[1], zd[3], zd[2]]), ("y", [yd[1], yd[3], yd[2]]), ("x", [xd[1], xd[3], xd[2]])]

    def ss_sends(st):
        ax, devices = stages[st]
        return [(f"ss{st}{i}", "ss", 0.01, lambda st=st, i=i, d=d: (sst.at[st], ssb.at[st, i], d)) for i, d in enumerate(devices)]

    def ss_add(st):
        tot = sst[st]
        for i in range(len(stages[st][1])):
            tot = tot + ssb[st, i]
        sst[st + 1] = tot

    add("ss0", 0.1, 2, deps=["pre1", "pre2", "pre3"], sends=ss_sends(0))
    for st in range(4):
        add(f"ss{st + 1}", 0.1, 2, lambda st=st: ss_add(st), waits=[f"ss{st}{i}" for i in range(len(stages[st][1]))],
            sends=ss_sends(st + 1) if st < 3 else [])

    def ag_done():
        for c in lbs:
            c.wait()

    add("agd", 0.1, 1, ag_done, deps=[f"ag{k}" for k in range(4)] + [f"{ax}f{s}{k}" for ax in "xy" for s in "RL" for k in range(4)]
        + [f"core{j}{k}" for j in (1, 2, 3) for k in range(4)],
        waits=[f"y{n}{k}" for n in ("R1", "L0", "FR", "FL") for k in range(4)] + [f"c{j}{k}" for j in range(4) for k in range(4)])

    def factor():
        return rms_target * math.sqrt(M) / (jnp.sqrt(sst[4][0:1, 0:1]) + 1e-07)

    def ring(tag, ax, pos, rd, part, r1, r2, full, w, prios, compute, comp_cost, comp_deps, add_cost, finish, comp_waits=()):
        def q(k):
            return (pos + k) % 4

        up, down = ax + "+", ax + "-"
        add(tag + "0", comp_cost, prios[0], compute, deps=comp_deps, waits=comp_waits, sends=[
            (tag + "A", up, w, lambda: (part(q(2), 0), r1(0), rd[1])),
            (tag + "B", down, w, lambda: (part(q(2), 1), r1(1), rd[3])),
            (tag + "C", up, w, lambda: (part(q(1), 1), r2(0, 1), rd[1])),
            (tag + "D", down, w, lambda: (part(q(3), 0), r2(1, 0), rd[3]))])

        def accumulate(k, hh):
            ref = part(q(k), hh)
            ref[...] = (ref[...].astype(F32) + r1(hh)[...].astype(F32)).astype(BF)

        add(tag + "1a", add_cost, prios[1], lambda: accumulate(1, 0), waits=[tag + "A"], sends=[
            (tag + "E", up, w, lambda: (part(q(1), 0), r2(0, 0), rd[1]))])
        add(tag + "1b", add_cost, prios[1], lambda: accumulate(3, 1), waits=[tag + "B"], sends=[
            (tag + "F", down, w, lambda: (part(q(3), 1), r2(1, 1), rd[3]))])

        def total():
            for hh in (0, 1):
                finish(hh, part(pos, hh)[...].astype(F32) + r2(0, hh)[...].astype(F32) + r2(1, hh)[...].astype(F32))

        sums = [tag + c for c in "CDEF"]
        if full is None:
            return total, sums
        add(tag + "2", 3 * add_cost, prios[2], total, waits=sums, sends=[
            (tag + "G", up, w, lambda: (full(pos, 0), full(pos, 0), rd[1])),
            (tag + "H", down, w, lambda: (full(pos, 1), full(pos, 1), rd[3])),
            (tag + "I", up, w, lambda: (full(pos, 1), full(pos, 1), rd[1])),
            (tag + "J", down, w, lambda: (full(pos, 0), full(pos, 0), rd[3]))],
            deps=["ss4"] if tag[0] == "g" else [])
        add(tag + "3a", 0.05, prios[3], waits=[tag + "G"], sends=[
            (tag + "K", up, w, lambda: (full(q(3), 0), full(q(3), 0), rd[1]))])
        add(tag + "3b", 0.05, prios[3], waits=[tag + "H"], sends=[
            (tag + "L", down, w, lambda: (full(q(1), 1), full(q(1), 1), rd[3]))])
        return [tag + c for c in "IJKL"], [tag + "3a", tag + "3b"]

    def tile(buf, t, half):
        return lambda q, hh: buf.at[pl.ds(al(t * TR + q * QR), QR), pl.ds(hh * half, half)]

    f_waits = []
    f_deps = []
    g_all = []
    for t in range(T):
        rows = pl.ds(t * TR, TR)

        def g_mm(rows=rows):
            gp[rows, :] = lax.dot_general(
                a_ref[rows, :], b_ref[...], (((1,), (1,)), ((), ())), preferred_element_type=F32).astype(BF)

        def f_mm(rows=rows):
            for j in range(2):
                fp[rows, halves[j]] = jnp.dot(gf[rows, :], b_ref[:, halves[j]], preferred_element_type=F32).astype(BF)

        def g_finish(hh, tot, t=t):
            f = factor()
            tile(gf, t, GH)(z, hh)[...] = (tot * jnp.broadcast_to(f * f, tot.shape)).astype(BF)

        def f_finish(hh, tot, t=t):
            d = a_ref[pl.ds(al(t * TR + y * QR), QR), halves[hh]].astype(F32)
            tile(hf, t, FH)(y, hh)[...] = (coef_b * d + coef_c * tot).astype(BF)

        gw, gd = ring(
            f"g{t}", "z", z, zd, tile(gp, t, GH), lambda hh, t=t: g1buf.at[t, hh], lambda s, hh, t=t: g2buf.at[t, s, hh],
            tile(gf, t, GH), us(QR, GH), (9 + t, 2 + t, 2 + t, 2 + t), g_mm, 17.5 / T,
            ["agd"] + ([f"g{t - WINDOW_G}2"] if t >= WINDOW_G else []), 0.1, g_finish)
        g_all.append(f"f{t}0")
        fw, fd = ring(
            f"f{t}", "y", y, yd, tile(fp, t, FH), lambda hh, t=t: f1buf.at[t, hh], lambda s, hh, t=t: f2buf.at[t, s, hh],
            tile(hf, t, FH), us(QR, FH), (5 + t, 1 + t, 1 + t, 1 + t), f_mm, 10.5 / T,
            gd + ([f"f{t - WINDOW_F}2"] if t >= WINDOW_F else []), 0.1, f_finish, comp_waits=gw)
        f_waits += fw
        f_deps += fd

    for c in range(AR // 128):
        def transpose(c=c):
            rows = pl.ds(c * 128, 128)
            gt[:, rows] = gf[rows, :].T

        need = [f"f{t}0" for t in range(T) if t * TR < (c + 1) * 128 and (t + 1) * TR > c * 128]
        add(f"tr{c}", 0.3, 20, transpose, deps=need)
    add("hd", 0.0, 0, deps=f_deps + [f"tr{c}" for c in range(AR // 128)], waits=f_waits)

    own_out = []
    for n in range(NT):
        ns = pl.ds(n * NW, NW)

        def s_mm(hb, n=n, ns=ns):
            tot = jnp.dot(gt[pl.ds(al(hb * AR), AR), :], hf[:, ns], preferred_element_type=F32).astype(BF)
            for i in range(RING):
                sp[n, hb, i] = tot[i * UNIT:(i + 1) * UNIT, :]

        def s_add(n=n):
            for i in range(RING):
                sp[n, h, i] = (sp[n, h, i].astype(F32) + sr[n, i].astype(F32)).astype(BF)

        def s_part(q, hh, n=n):
            return sp.at[n, h, q, pl.ds(hh * UH, UH), :]

        def s_finish(hh, tot, n=n, ns=ns):
            d = a_ref[pl.ds(al(y * UNIT + hh * UH), UH), ns].astype(F32)
            u = (coef_a * d + tot) * jnp.broadcast_to(factor() * scale_out, tot.shape)
            ub[pl.ds(hh * UH, UH), ns] = u.astype(BF)

        add(f"s{n}x", 0.75, 9 + n, lambda s_mm=s_mm: s_mm(1 - h), deps=["hd"] + ([f"s{n - WINDOW_S}1a"] if n >= WINDOW_S else []), sends=[
            (f"s{n}X", "c", AR * NW * 2 * CORE_US, lambda n=n: (sp.at[n, 1 - h], sr.at[n], partner))])
        add(f"s{n}y", 0.75, 8 + n, lambda s_mm=s_mm: s_mm(h), deps=[f"s{n}x"])
        total, sums = ring(
            f"s{n}", "x", x, xd, s_part, lambda hh, n=n: s1buf.at[n, hh], lambda s, hh, n=n: s2buf.at[n, s, hh], None,
            us(UH, NW), (7, 1, 1, 1), s_add, 0.4, [f"s{n}y"], 0.1, s_finish, comp_waits=[f"s{n}X"])

        def oc(n):
            return pl.ds(al(z * KB + n * NW, 128), NW)

        def fin(total=total, n=n, ns=ns):
            total()
            c = pltpu.make_async_copy(ub.at[pl.ds(al(z * ROWS), ROWS), ns], out_ref.at[:, oc(n)], lsem.at[16 + n])
            c.start()
            own_out.append(c)

        add(f"s{n}2", 0.4, 0, fin, waits=sums, sends=[
            (f"o{n}{k}", "z-" if k == 3 else "z+", us(ROWS, NW) * (2 if k == 2 else 1),
             lambda n=n, k=k, ns=ns: (ub.at[pl.ds(al(((z + k) % 4) * ROWS), ROWS), ns], out_ref.at[:, oc(n)], zd[k]))
            for k in (2, 1, 3)])

    sched = order_of(tasks)
    if SHOW:
        SHOW(sched)
    for k, _, _ in sched:
        for w in k.waits:
            copies[w].wait_recv()
            waited.add(w)
        if k.fn is not None:
            k.fn()
        for name, _, _, make in k.sends:
            issue(name, *make())

    for name, c in copies.items():
        if name not in waited:
            c.wait_recv()
    for c in own_out + stores:
        c.wait()
    for c in copies.values():
        c.wait_send()


def muon(grad, momentum):
    def v(*shape):
        return pltpu.VMEM(shape, BF)

    hbm = pl.BlockSpec(memory_space=pl.ANY)
    return pl.pallas_call(
        kernel,
        out_shape=(jax.ShapeDtypeStruct((ROWS, N), BF), jax.ShapeDtypeStruct((ROWS, N), F32)),
        in_specs=[hbm, hbm],
        out_specs=(hbm, hbm),
        scratch_shapes=[
            pltpu.VMEM((RING, ROWS, KB), F32), pltpu.VMEM((RING, ROWS, KB), F32), v(RING, ROWS, KB),
            v(AR, KB), v(BR, KB),
            v(AR, BR), v(T, 2, QR, GH), v(T, 2, 2, QR, GH), v(AR, BR), v(BR, AR),
            v(AR, KB), v(T, 2, QR, FH), v(T, 2, 2, QR, FH), v(AR, KB),
            v(NT, 2, RING, UNIT, NW), v(NT, RING, UNIT, NW), v(NT, 2, UH, NW), v(NT, 2, 2, UH, NW),
            v(UNIT, KB),
            pltpu.VMEM((4, 3, 8, 128), F32), pltpu.VMEM((5, 8, 128), F32),
            pltpu.SemaphoreType.DMA((N_SEM,)), pltpu.SemaphoreType.DMA((N_SEM,)), pltpu.SemaphoreType.DMA((16 + NT,)),
        ],
        compiler_params=pltpu.CompilerParams(collective_id=0, has_side_effects=True, vmem_limit_bytes=63 << 20),
    )(grad, momentum)


def solution(mesh):
    return jax.shard_map(
        muon,
        mesh=mesh,
        in_specs=(P(("row", "col"), None), P(("row", "col"), None)),
        out_specs=(P(("row", "col"), None), P(("row", "col"), None)),
        check_vma=False,
    )
```

```python
import math

import jax
import jax.numpy as jnp
from jax import lax
from jax.experimental import pallas as pl
from jax.experimental.pallas import tpu as pltpu
from jax.sharding import PartitionSpec as P

M = 7168
N = 8192

momentum_coef = 0.95
rms_target = 0.4
coef_a = 3.4445
coef_b = -4.775
coef_c = 2.0315
scale_out = 0.2 * math.sqrt(max(M, N))

BF = jnp.bfloat16
F32 = jnp.float32
MESH = pl.DeviceIdType.MESH

RING = 4
ROWS = 56
UNIT = RING * ROWS
KB = N // RING
AR = RING * UNIT
BR = 2 * AR
T = 4
TR = AR // T
QR = TR // RING
CT = 2
GW = BR // CT
G_SEQ = ((0, 0), (0, 1), (1, 0), (2, 0), (3, 0), (1, 1), (2, 1), (3, 1))
G_WIDE = 512
FH = KB // 2
N1 = 1024
N2 = KB - N1
F1H = N1 // 2
W2 = 512
P2 = N2 // W2
Q2 = GW // 2 // RING
NW = 256
NT = KB // NW
S1 = N1 // NW
UH = UNIT // 2
N_SEM = 400
WINDOW_G = 2
WINDOW_F = 4
WINDOW_P = 2
WINDOW_S = 2

LINK_US = 1e6 / 44.5e9
CORE_US = 1e6 / 500e9
HOP_US = 1.7
SHOW = None
AXIS = {1: "{0}+", 3: "{0}-", 2: "{0}+ {0}-"}


class Task:
    def __init__(self, name, cost, prio, fn=None, waits=(), sends=(), deps=()):
        self.name, self.cost, self.prio, self.fn = name, cost, prio, fn
        self.waits, self.sends, self.deps = list(waits), list(sends), list(deps)


def order_of(tasks):
    now, free, arrive, done, order = 0.0, {}, {}, set(), []
    todo = list(tasks)
    while todo:
        best = None
        for i, k in enumerate(todo):
            if any(d not in done for d in k.deps) or any(w not in arrive for w in k.waits):
                continue
            ready = max([arrive[w] for w in k.waits], default=0.0)
            key = (max(ready, now), k.prio, i)
            if best is None or key < best[0]:
                best = (key, k)
        key, k = best
        todo.remove(k)
        now = key[0] + k.cost
        for name, links, us, _ in k.sends:
            fin = now
            for link in links.split():
                free[link] = max(now, free.get(link, 0.0)) + us
                fin = max(fin, free[link])
            arrive[name] = fin + HOP_US
        done.add(k.name)
        order.append((k, key[0], now))
    return order


def kernel(grad_ref, mom_ref, out_ref, nm_ref, gin, minb, dbuf, a_ref, b_ref, gp, g1buf, g2buf, gf, gt, fp, f1buf, f2buf, hf,
           pp, pr, p1buf, p2buf, hp, sp, sr, vp, s1buf, s2buf, ub, ssb, sst, send, recv, lsem):
    row = lax.axis_index("row")
    col = lax.axis_index("col")
    x = row % 4
    h = col % 2
    y = (col // 2) % 4
    z = (col // 8) * 2 + row // 4

    def dev(dx=0, dy=0, dz=0, dh=0):
        nx, ny, nz, nh = (x + dx) % 4, (y + dy) % 4, (z + dz) % 4, (h + dh) % 2
        return {"row": (nz % 2) * 4 + nx, "col": (nz // 2) * 8 + ny * 2 + nh}

    zd = {k: dev(dz=k) for k in (1, 2, 3)}
    yd = {k: dev(dy=k) for k in (1, 2, 3)}
    xd = {k: dev(dx=k) for k in (1, 2, 3)}
    partner = dev(dh=1)

    def al(v, m=8):
        return pl.multiple_of(v, m)

    def cols(k):
        return pl.ds(al(((z + k) % 4) * KB, 128), KB)

    loads = {}
    for k in (0, 1, 3, 2):
        loads[k] = [pltpu.make_async_copy(grad_ref.at[:, cols(k)], gin.at[k], lsem.at[2 * k]),
                    pltpu.make_async_copy(mom_ref.at[:, cols(k)], minb.at[k], lsem.at[2 * k + 1])]
        for c in loads[k]:
            c.start()

    barrier = pltpu.get_barrier_semaphore()
    peers = [partner] + [r[k] for r in (zd, yd, xd) for k in (1, 2, 3)]
    for p in peers:
        pl.semaphore_signal(barrier, inc=1, device_id=p, device_id_type=MESH)

    copies = {}
    waited = set()

    def issue(name, src, dst, device):
        i = len(copies)
        c = pltpu.make_async_remote_copy(
            src_ref=src, dst_ref=dst, send_sem=send.at[i], recv_sem=recv.at[i], device_id=device, device_id_type=MESH)
        c.start()
        copies[name] = c

    tasks = []

    def add(*args, **kw):
        tasks.append(Task(*args, **kw))

    def us(rows, columns):
        return rows * columns * 2 * LINK_US

    def unit_rows(i):
        return pl.ds(al(i * UNIT), UNIT)

    def piece(unit, k):
        return pl.ds(al(unit * UNIT + ((z + k) % 4) * ROWS), ROWS)

    stores = []

    def pre(k):
        for c in loads[k]:
            c.wait()
        g = gin[k]
        nm = momentum_coef * minb[k] + g
        d = g + momentum_coef * nm
        minb[k] = nm
        c = pltpu.make_async_copy(minb.at[k], nm_ref.at[:, cols(k)], lsem.at[8 + k])
        c.start()
        stores.append(c)
        if k == 0:
            a_ref[piece(y, 0), :] = d.astype(BF)
        else:
            dbuf[k] = d.astype(BF)
        s = jnp.sum(jnp.sum(d * d, axis=0, keepdims=True), axis=1, keepdims=True)
        s = jnp.broadcast_to(s, (8, 128))
        sst[0] = s if k == 0 else sst[0] + s

    pre(0)
    pl.semaphore_wait(barrier, len(peers))

    halves = (pl.ds(0, FH), pl.ds(FH, FH))

    def bunit(k):
        return h * 4 + (x + k) % 4

    def aunit(k):
        return (y + k) % 4

    lbs = []

    def ag_sends(k):
        pa, pb = piece(y, k), piece(h * 4 + x, k)
        w = us(ROWS, FH)
        out = []
        for hr, hl in ((0, 1), (1, 0)):
            for ax, rd, ref, rows in (("y", yd, a_ref, pa), ("x", xd, b_ref, pb)):
                out.append((f"{ax}R{hr}{k}", ax + "+", w, lambda hh=hr, rd=rd, ref=ref, rows=rows: (
                    a_ref.at[pa, halves[hh]], ref.at[rows, halves[hh]], rd[1])))
                out.append((f"{ax}L{hl}{k}", ax + "-", w, lambda hh=hl, rd=rd, ref=ref, rows=rows: (
                    a_ref.at[pa, halves[hh]], ref.at[rows, halves[hh]], rd[3])))
        out.append((f"c0{k}", "c", ROWS * KB * 2 * CORE_US, lambda: (a_ref.at[pa, :], b_ref.at[pb, :], partner)))
        return out

    def local_b(k):
        c = pltpu.make_async_copy(a_ref.at[piece(y, k), :], b_ref.at[piece(h * 4 + x, k), :], lsem.at[12 + k])
        c.start()
        lbs.append(c)

    def cp(ref, rows, hh, device):
        return lambda: (ref.at[rows, hh], ref.at[rows, hh], device)

    add("ag0", 0.1, 0, lambda: local_b(0), sends=ag_sends(0))
    for k in (1, 3, 2):
        add(f"pre{k}", 0.5, 1, lambda k=k: pre(k), sends=[
            (f"z{k}", AXIS[k].format("z"), us(ROWS, KB),
             lambda k=k: (dbuf.at[k], a_ref.at[piece(y, 0), :], zd[k]))])
    for k, src in ((3, 1), (1, 3), (2, 2)):
        add(f"ag{k}", 0.1, 0, lambda k=k: local_b(k), waits=[f"z{src}"], sends=ag_sends(k))
    for k in (0, 3, 1, 2):
        w = us(ROWS, FH)
        for ax, rd, ref, un in (("y", yd, a_ref, aunit), ("x", xd, b_ref, bunit)):
            add(f"{ax}fR{k}", 0.05, 0, waits=[f"{ax}R0{k}"], sends=[
                (f"{ax}FR{k}", ax + "+", w, lambda k=k, rd=rd, ref=ref, un=un: cp(ref, piece(un(3), k), halves[0], rd[1])())])
            add(f"{ax}fL{k}", 0.05, 0, waits=[f"{ax}L1{k}"], sends=[
                (f"{ax}FL{k}", ax + "-", w, lambda k=k, rd=rd, ref=ref, un=un: cp(ref, piece(un(1), k), halves[1], rd[3])())])
        for j, ws, ds in ((3, [f"xR1{k}"], [f"xfR{k}"]), (1, [f"xL0{k}"], [f"xfL{k}"]), (2, [f"xFR{k}", f"xFL{k}"], [])):
            add(f"core{j}{k}", 0.05, 1, waits=ws, deps=ds, sends=[
                (f"c{j}{k}", "c", ROWS * KB * 2 * CORE_US,
                 lambda j=j, k=k: cp(b_ref, piece(bunit(j), k), pl.ds(0, KB), partner)())])

    stages = [("c", [partner]), ("z", [zd[1], zd[3], zd[2]]), ("y", [yd[1], yd[3], yd[2]]), ("x", [xd[1], xd[3], xd[2]])]

    def ss_sends(st):
        ax, devices = stages[st]
        return [(f"ss{st}{i}", ax if ax == "c" else AXIS[(1, 3, 2)[i]].format(ax), 0.01, lambda st=st, i=i, d=d: (sst.at[st], ssb.at[st, i], d)) for i, d in enumerate(devices)]

    def ss_add(st):
        tot = sst[st]
        for i in range(len(stages[st][1])):
            tot = tot + ssb[st, i]
        sst[st + 1] = tot

    add("ss0", 0.1, 2, deps=["pre1", "pre2", "pre3"], sends=ss_sends(0))
    for st in range(4):
        add(f"ss{st + 1}", 0.1, 2, lambda st=st: ss_add(st), waits=[f"ss{st}{i}" for i in range(len(stages[st][1]))],
            sends=ss_sends(st + 1) if st < 3 else [])

    def ag_done():
        for c in lbs:
            c.wait()

    add("agd", 0.1, 1, ag_done, deps=[f"ag{k}" for k in range(4)] + [f"{ax}f{s}{k}" for ax in "xy" for s in "RL" for k in range(4)]
        + [f"core{j}{k}" for j in (1, 2, 3) for k in range(4)],
        waits=[f"y{n}{k}" for n in ("R1", "L0", "FR", "FL") for k in range(4)] + [f"c{j}{k}" for j in range(4) for k in range(4)])

    def factor():
        return rms_target * math.sqrt(M) / (jnp.sqrt(sst[4][0:1, 0:1]) + 1e-07)

    def ring(tag, ax, pos, rd, part, r1, r2, full, w, prios, compute, comp_cost, comp_deps, add_cost, finish, comp_waits=(),
             sum_deps=(), sum_sends=()):
        def q(k):
            return (pos + k) % 4

        up, down = ax + "+", ax + "-"
        add(tag + "0", comp_cost, prios[0], compute, deps=comp_deps, waits=comp_waits, sends=[
            (tag + "A", up, w[0], lambda: (part(q(2), 0), r1(0), rd[1])),
            (tag + "B", down, w[1], lambda: (part(q(2), 1), r1(1), rd[3])),
            (tag + "C", up, w[1], lambda: (part(q(1), 1), r2(0, 1), rd[1])),
            (tag + "D", down, w[0], lambda: (part(q(3), 0), r2(1, 0), rd[3]))])

        def accumulate(k, hh):
            ref = part(q(k), hh)
            ref[...] = (ref[...].astype(F32) + r1(hh)[...].astype(F32)).astype(BF)

        add(tag + "1a", add_cost, prios[1], lambda: accumulate(1, 0), waits=[tag + "A"], sends=[
            (tag + "E", up, w[0], lambda: (part(q(1), 0), r2(0, 0), rd[1]))])
        add(tag + "1b", add_cost, prios[1], lambda: accumulate(3, 1), waits=[tag + "B"], sends=[
            (tag + "F", down, w[1], lambda: (part(q(3), 1), r2(1, 1), rd[3]))])

        def total():
            for hh in (0, 1):
                finish(hh, part(pos, hh)[...].astype(F32) + r2(0, hh)[...].astype(F32) + r2(1, hh)[...].astype(F32))

        sums = [tag + c for c in "CDEF"]
        if full is None:
            return total, sums
        add(tag + "2", 3 * add_cost, prios[2], total, waits=sums, sends=[
            (tag + "G", up, w[0], lambda: (full(pos, 0), full(pos, 0), rd[1])),
            (tag + "H", down, w[1], lambda: (full(pos, 1), full(pos, 1), rd[3])),
            (tag + "I", up, w[1], lambda: (full(pos, 1), full(pos, 1), rd[1])),
            (tag + "J", down, w[0], lambda: (full(pos, 0), full(pos, 0), rd[3]))] + list(sum_sends), deps=list(sum_deps))
        add(tag + "3a", 0.05, prios[3], waits=[tag + "G"], sends=[
            (tag + "K", up, w[0], lambda: (full(q(3), 0), full(q(3), 0), rd[1]))])
        add(tag + "3b", 0.05, prios[3], waits=[tag + "H"], sends=[
            (tag + "L", down, w[1], lambda: (full(q(1), 1), full(q(1), 1), rd[3]))])
        return [tag + c for c in "IJKL"], [tag + "3a", tag + "3b"]

    g_waits = {}
    g_deps = {}
    for b, (t, c) in enumerate(G_SEQ):
        rows, gcols = pl.ds(t * TR, TR), pl.ds(c * GW, GW)
        cut = G_WIDE if b % 2 == 0 else GW - G_WIDE
        spans = ((0, cut), (cut, GW - cut))

        def g_mm(rows=rows, gcols=gcols):
            gp[rows, gcols] = lax.dot_general(
                a_ref[rows, :], b_ref[gcols, :], (((1,), (1,)), ((), ())), preferred_element_type=F32).astype(BF)

        def g_part(buf, t=t, c=c, spans=spans):
            return lambda q, hh: buf.at[pl.ds(al(t * TR + q * QR), QR), pl.ds(c * GW + spans[hh][0], spans[hh][1])]

        def g_finish(hh, tot, full=g_part(gf)):
            f = factor()
            full(z, hh)[...] = (tot * jnp.broadcast_to(f * f, tot.shape)).astype(BF)

        prev = [f"g{G_SEQ[b - WINDOW_G][0]}{G_SEQ[b - WINDOW_G][1]}2"] if b >= WINDOW_G else []
        g_waits[t, c], g_deps[t, c] = ring(
            f"g{t}{c}", "z", z, zd, g_part(gp),
            lambda hh, b=b, spans=spans: g1buf.at[b, hh, :, pl.ds(0, spans[hh][1])],
            lambda s, hh, b=b, spans=spans: g2buf.at[b, s, hh, :, pl.ds(0, spans[hh][1])],
            g_part(gf), [us(QR, w) for _, w in spans], (30 + b, 2 + b, 2 + b, 2 + b), g_mm, 13.0 / len(G_SEQ),
            ["agd"] + prev, 0.15, g_finish, sum_deps=["ss4"])

    def g_ready(t, c):
        name = f"gd{t}{c}"

        def transpose(t=t, c=c):
            rows, gcols = pl.ds(t * TR, TR), pl.ds(c * GW, GW)
            gt[t, gcols, :] = gf[rows, gcols].T

        add(name, 0.4, 12, transpose, waits=g_waits[t, c], deps=g_deps[t, c])
        return name

    ready = {(t, c): g_ready(t, c) for t, c in G_SEQ}

    f_waits = []
    f_deps = []
    for t in range(T):
        rows = pl.ds(t * TR, TR)

        def f_mm(rows=rows):
            def body(j, carry):
                js = pl.ds(al(j * 512, 512), 512)
                fp[rows, js] = jnp.dot(gf[rows, :], b_ref[:, js], preferred_element_type=F32).astype(BF)
                return carry

            lax.fori_loop(0, N1 // 512, body, 0)

        def f_part(buf, t=t):
            return lambda q, hh: buf.at[pl.ds(al(t * TR + q * QR), QR), pl.ds(hh * F1H, F1H)]

        def f_finish(hh, tot, t=t, full=f_part(hf)):
            d = a_ref[pl.ds(al(t * TR + y * QR), QR), pl.ds(hh * F1H, F1H)].astype(F32)
            full(y, hh)[...] = (coef_b * d + coef_c * tot).astype(BF)

        fw, fd = ring(
            f"f{t}", "y", y, yd, f_part(fp), lambda hh, t=t: f1buf.at[t, hh], lambda s, hh, t=t: f2buf.at[t, s, hh],
            f_part(hf), [us(QR, F1H)] * 2, (15 + t, 1 + t, 1 + t, 1 + t), f_mm, 7.0 / T,
            [ready[t, c] for c in range(CT)] + ([f"f{t - WINDOW_F}2"] if t >= WINDOW_F else []), 0.15, f_finish)
        f_waits += fw
        f_deps += fd

    CORE_ROWS = GW // 2
    p_waits = []
    p_deps = []
    p_names = []
    for c in range(CT):
        for j in range(P2):
            js = pl.ds(j * W2, W2)

            def p_rows(hb, c=c):
                return pl.ds(al(c * GW + hb * CORE_ROWS), CORE_ROWS)

            def p_mm(hb, c=c, j=j, p_rows=p_rows):
                acc = jnp.zeros((CORE_ROWS, W2), F32)
                for t in range(T):
                    acc = acc + jnp.dot(gt[t, p_rows(hb), :], a_ref[pl.ds(t * TR, TR), pl.ds(N1 + j * W2, W2)],
                                        preferred_element_type=F32)
                pp[p_rows(hb), pl.ds(j * W2, W2)] = acc.astype(BF)

            tag = f"p{c}{j}"
            i = len(p_names)
            p_names.append(tag)
            prev = [f"{p_names[i - WINDOW_P]}2"] if i >= WINDOW_P else []
            add(tag + "x", 3.5 / CT / P2, 20 + i, lambda p_mm=p_mm: p_mm(1 - h), deps=[ready[t, c] for t in range(T)] + prev, sends=[
                (tag + "X", "c", CORE_ROWS * W2 * 2 * CORE_US, lambda p_rows=p_rows, js=js, c=c, j=j: (
                    pp.at[p_rows(1 - h), js], pr.at[c, j], partner))])
            add(tag + "y", 3.5 / CT / P2, 19 + i, lambda p_mm=p_mm: p_mm(h), deps=[tag + "x"])

            def p_add(p_rows=p_rows, js=js, c=c, j=j):
                r = p_rows(h)
                pp[r, js] = (pp[r, js].astype(F32) + pr[c, j].astype(F32)).astype(BF)

            def p_part(buf, c=c, j=j):
                return lambda q, hh: buf.at[pl.ds(al(c * GW + h * CORE_ROWS + q * Q2), Q2), pl.ds(j * W2 + hh * (W2 // 2), W2 // 2)]

            def p_quarter(k, c=c, js=js):
                ref = hp.at[pl.ds(al(c * GW + h * CORE_ROWS + (x + k) % 4 * Q2), Q2), js]
                return ref, ref, partner

            def p_finish(hh, tot, c=c, j=j, full=p_part(hp)):
                d = b_ref[pl.ds(al(c * GW + h * CORE_ROWS + x * Q2), Q2), pl.ds(N1 + j * W2 + hh * (W2 // 2), W2 // 2)].astype(F32)
                full(x, hh)[...] = (coef_b * d + coef_c * tot).astype(BF)

            core_us = Q2 * W2 * 2 * CORE_US
            pw, pd = ring(
                tag, "x", x, xd, p_part(pp), lambda hh, c=c, j=j: p1buf.at[c, j, hh], lambda s, hh, c=c, j=j: p2buf.at[c, j, s, hh],
                p_part(hp), [us(Q2, W2 // 2)] * 2, (3 + i, 1, 1, 1), p_add, 0.3, [tag + "y"], 0.2, p_finish,
                comp_waits=[tag + "X"], sum_sends=[(tag + "q0", "c", core_us, lambda p_quarter=p_quarter: p_quarter(0))])
            for k, ws, ds in ((3, pw[0:1], pd[0:1]), (1, pw[1:2], pd[1:2]), (2, pw[2:], [])):
                add(f"{tag}c{k}", 0.05, 1, waits=ws, deps=ds, sends=[
                    (f"{tag}q{k}", "c", core_us, lambda p_quarter=p_quarter, k=k: p_quarter(k))])
            p_waits += [f"{tag}q{k}" for k in range(4)]
            p_deps += pd + [f"{tag}c{k}" for k in (1, 2, 3)]

    add("hd", 0.0, 0, deps=f_deps + [ready[k] for k in ready], waits=f_waits)
    add("hpd", 0.0, 0, deps=p_deps + [ready[k] for k in ready], waits=p_waits)

    own_out = []

    def send_back(tag, n, total, sums):
        ns = pl.ds(n * NW, NW)
        oc = pl.ds(al(z * KB + n * NW, 128), NW)

        def fin():
            total()
            c = pltpu.make_async_copy(ub.at[pl.ds(al(z * ROWS), ROWS), ns], out_ref.at[:, oc], lsem.at[16 + n])
            c.start()
            own_out.append(c)

        add(tag + "2", 0.4, 0, fin, waits=sums, sends=[
            (f"o{n}{k}", AXIS[k].format("z"), us(ROWS, NW),
             lambda k=k: (ub.at[pl.ds(al(((z + k) % 4) * ROWS), ROWS), ns], out_ref.at[:, oc], zd[k]))
            for k in (2, 1, 3)])

    for n in range(NT):
        ns = pl.ds(n * NW, NW)
        tag = f"s{n}"

        def s_finish(hh, tot, ns=ns):
            d = a_ref[pl.ds(al(y * UNIT + hh * UH), UH), ns].astype(F32)
            u = (coef_a * d + tot) * jnp.broadcast_to(factor() * scale_out, tot.shape)
            ub[pl.ds(hh * UH, UH), ns] = u.astype(BF)

        bufs = (lambda hh, n=n: s1buf.at[n, hh], lambda s, hh, n=n: s2buf.at[n, s, hh])
        if n < S1:
            def s_mm(hb, n=n, ns=ns):
                r = pl.ds(al(hb * AR), AR)
                acc = jnp.zeros((AR, NW), F32)
                for t in range(T):
                    acc = acc + jnp.dot(gt[t, r, :], hf[pl.ds(t * TR, TR), ns], preferred_element_type=F32)
                tot = acc.astype(BF)
                for i in range(RING):
                    sp[n, hb, i] = tot[i * UNIT:(i + 1) * UNIT, :]

            def s_add(n=n):
                for i in range(RING):
                    sp[n, h, i] = (sp[n, h, i].astype(F32) + sr[n, i].astype(F32)).astype(BF)

            prev = [f"s{n - WINDOW_S}1a"] if n >= WINDOW_S else []
            add(tag + "x", 0.75, 40 + n, lambda s_mm=s_mm: s_mm(1 - h), deps=["hd"] + prev, sends=[
                (tag + "X", "c", AR * NW * 2 * CORE_US, lambda n=n: (sp.at[n, 1 - h], sr.at[n], partner))])
            add(tag + "y", 0.75, 39 + n, lambda s_mm=s_mm: s_mm(h), deps=[tag + "x"])
            total, sums = ring(
                tag, "x", x, xd, lambda q, hh, n=n: sp.at[n, h, q, pl.ds(hh * UH, UH), :], *bufs, None,
                [us(UH, NW)] * 2, (7, 1, 1, 1), s_add, 0.4, [tag + "y"], 0.1, s_finish, comp_waits=[tag + "X"])
        else:
            m = n - S1

            def v_mm(m=m):
                tot = jnp.dot(gf[...], hp[:, pl.ds(m * NW, NW)], preferred_element_type=F32).astype(BF)
                for i in range(RING):
                    vp[m, i] = tot[i * UNIT:(i + 1) * UNIT, :]

            prev = [f"s{n - WINDOW_S}1a"] if m >= WINDOW_S else []
            total, sums = ring(
                tag, "y", y, yd, lambda q, hh, m=m: vp.at[m, q, pl.ds(hh * UH, UH), :], *bufs, None,
                [us(UH, NW)] * 2, (40 + m, 1, 1, 1), v_mm, 1.4, ["hpd"] + prev, 0.1, s_finish)
        send_back(tag, n, total, sums)

    sched = order_of(tasks)
    if SHOW:
        SHOW(sched)
    for k, _, _ in sched:
        for w in k.waits:
            copies[w].wait_recv()
            waited.add(w)
        if k.fn is not None:
            k.fn()
        for name, _, _, make in k.sends:
            issue(name, *make())

    for name, c in copies.items():
        if name not in waited:
            c.wait_recv()
    for c in own_out + stores:
        c.wait()
    for c in copies.values():
        c.wait_send()


def muon(grad, momentum):
    def v(*shape):
        return pltpu.VMEM(shape, BF)

    hbm = pl.BlockSpec(memory_space=pl.ANY)
    return pl.pallas_call(
        kernel,
        out_shape=(jax.ShapeDtypeStruct((ROWS, N), BF), jax.ShapeDtypeStruct((ROWS, N), F32)),
        in_specs=[hbm, hbm],
        out_specs=(hbm, hbm),
        scratch_shapes=[
            pltpu.VMEM((RING, ROWS, KB), F32), pltpu.VMEM((RING, ROWS, KB), F32), v(RING, ROWS, KB),
            v(AR, KB), v(BR, KB),
            v(AR, BR), v(T * CT, 2, QR, G_WIDE), v(T * CT, 2, 2, QR, G_WIDE), v(AR, BR), v(T, BR, TR),
            v(AR, N1), v(T, 2, QR, F1H), v(T, 2, 2, QR, F1H), v(AR, N1),
            v(BR, N2), v(CT, P2, GW // 2, W2), v(CT, P2, 2, Q2, W2 // 2), v(CT, P2, 2, 2, Q2, W2 // 2), v(BR, N2),
            v(S1, 2, RING, UNIT, NW), v(S1, RING, UNIT, NW), v(NT - S1, RING, UNIT, NW), v(NT, 2, UH, NW), v(NT, 2, 2, UH, NW),
            v(UNIT, KB),
            pltpu.VMEM((4, 3, 8, 128), F32), pltpu.VMEM((5, 8, 128), F32),
            pltpu.SemaphoreType.DMA((N_SEM,)), pltpu.SemaphoreType.DMA((N_SEM,)), pltpu.SemaphoreType.DMA((16 + NT,)),
        ],
        compiler_params=pltpu.CompilerParams(collective_id=0, has_side_effects=True, vmem_limit_bytes=63 << 20),
    )(grad, momentum)


def solution(mesh):
    return jax.shard_map(
        muon,
        mesh=mesh,
        in_specs=(P(("row", "col"), None), P(("row", "col"), None)),
        out_specs=(P(("row", "col"), None), P(("row", "col"), None)),
        check_vma=False,
    )
```

```python
import math

import jax
import jax.numpy as jnp
from jax import lax
from jax.experimental import pallas as pl
from jax.experimental.pallas import tpu as pltpu
from jax.sharding import PartitionSpec as P

M = 7168
N = 8192

momentum_coef = 0.95
rms_target = 0.4
coef_a = 3.4445
coef_b = -4.775
coef_c = 2.0315
scale_out = 0.2 * math.sqrt(max(M, N))

BF = jnp.bfloat16
F32 = jnp.float32
MESH = pl.DeviceIdType.MESH

RING = 4
ROWS = 56
UNIT = RING * ROWS
KB = N // RING
AR = RING * UNIT
BR = 2 * AR
T = 4
TR = AR // T
QR = TR // RING
C_W = (768, 768, 256)
C_0 = (0, 768, 1536)
CT = len(C_W)
CW_MAX = max(C_W)
G_SEQ = ((0, 0), (1, 0), (2, 0), (3, 0), (0, 1), (0, 2), (1, 1), (1, 2), (2, 1), (3, 1), (2, 2), (3, 2))
FH = KB // 2
N1 = 1024
N2 = KB - N1
F1H = N1 // 2
W2 = 512
P2 = N2 // W2
NW = 256
NT = KB // NW
S1 = N1 // NW
UH = UNIT // 2
N_SEM = 480
WINDOW_G = 4
WINDOW_F = 4
WINDOW_P = 4
WINDOW_S = 4

LINK_US = 1e6 / 44.5e9
CORE_US = 1e6 / 500e9
HOP_US = 2.5
COST_SCALE = 1.5
COST_EACH = 0.1
SHOW = None
AXIS = {1: "{0}+", 3: "{0}-", 2: "{0}+ {0}-"}


class Task:
    def __init__(self, name, cost, prio, fn=None, waits=(), sends=(), deps=(), after=()):
        self.name, self.cost, self.prio, self.fn = name, cost, prio, fn
        self.waits, self.sends, self.deps, self.after = list(waits), list(sends), list(deps), list(after)


def order_of(tasks):
    now, free, arrive, done, order = 0.0, {}, {}, set(), []
    todo = list(tasks)
    while todo:
        best = None
        for i, k in enumerate(todo):
            if any(d not in done for d in k.deps) or any(w not in arrive for w in k.waits + k.after):
                continue
            ready = max([arrive[w] for w in k.waits + k.after], default=0.0)
            key = (max(ready, now), k.prio, i)
            if best is None or key < best[0]:
                best = (key, k)
        key, k = best
        todo.remove(k)
        now = key[0] + k.cost * COST_SCALE + COST_EACH
        for name, links, us, _ in k.sends:
            fin = now
            for link in links.split():
                free[link] = max(now, free.get(link, 0.0)) + us
                fin = max(fin, free[link])
            arrive[name] = fin + HOP_US
        done.add(k.name)
        order.append((k, key[0], now))
    return order


def kernel(grad_ref, mom_ref, out_ref, nm_ref, gin, minb, dbuf, a_ref, b_ref, gp, g1buf, g2buf, gf, gt, fp, f1buf, f2buf, hf,
           pp, pr, p1buf, p2buf, hp, sp, sr, vp, s1buf, s2buf, ub, ssb, sst, send, recv, lsem, zsem):
    row = lax.axis_index("row")
    col = lax.axis_index("col")
    x = row % 4
    h = col % 2
    y = (col // 2) % 4
    z = (col // 8) * 2 + row // 4

    def dev(dx=0, dy=0, dz=0, dh=0):
        nx, ny, nz, nh = (x + dx) % 4, (y + dy) % 4, (z + dz) % 4, (h + dh) % 2
        return {"row": (nz % 2) * 4 + nx, "col": (nz // 2) * 8 + ny * 2 + nh}

    zd = {k: dev(dz=k) for k in (1, 2, 3)}
    yd = {k: dev(dy=k) for k in (1, 2, 3)}
    xd = {k: dev(dx=k) for k in (1, 2, 3)}
    partner = dev(dh=1)

    def al(v, m=8):
        return pl.multiple_of(v, m)

    def cols(k):
        return pl.ds(al(((z + k) % 4) * KB, 128), KB)

    loads = {}
    for k in (0, 1, 3, 2):
        loads[k] = [pltpu.make_async_copy(grad_ref.at[:, cols(k)], gin.at[k], lsem.at[2 * k]),
                    pltpu.make_async_copy(mom_ref.at[:, cols(k)], minb.at[k], lsem.at[2 * k + 1])]
        for c in loads[k]:
            c.start()

    barrier = pltpu.get_barrier_semaphore()
    peers = [partner] + [r[k] for r in (zd, yd, xd) for k in (1, 2, 3)]
    for p in peers:
        pl.semaphore_signal(barrier, inc=1, device_id=p, device_id_type=MESH)

    copies = {}
    waited = set()

    def issue(name, src, dst, device, recv_sem=None):
        i = len(copies)
        if recv_sem is not None:
            waited.add(name)
        c = pltpu.make_async_remote_copy(
            src_ref=src, dst_ref=dst, send_sem=send.at[i], recv_sem=recv.at[i] if recv_sem is None else recv_sem,
            device_id=device, device_id_type=MESH)
        c.start()
        copies[name] = c

    tasks = []

    def add(*args, **kw):
        tasks.append(Task(*args, **kw))

    def us(rows, columns):
        return rows * columns * 2 * LINK_US

    def slot(j):
        return z if j == 0 else j - 1 + (j + 3 - z) // 4

    def a_piece(unit, j):
        return pl.ds(al(slot(j) * UNIT + unit * ROWS), ROWS)

    def b_piece(unit, j):
        return pl.ds(al(slot(j) * 2 * UNIT + unit * ROWS), ROWS)

    stores = []

    def pre(k):
        for c in loads[k]:
            c.wait()
        g = gin[k]
        nm = momentum_coef * minb[k] + g
        d = g + momentum_coef * nm
        minb[k] = nm
        c = pltpu.make_async_copy(minb.at[k], nm_ref.at[:, cols(k)], lsem.at[8 + k])
        c.start()
        stores.append(c)
        if k == 0:
            a_ref[a_piece(y, 0), :] = d.astype(BF)
        else:
            dbuf[k] = d.astype(BF)
        s = jnp.sum(jnp.sum(d * d, axis=0, keepdims=True), axis=1, keepdims=True)
        s = jnp.broadcast_to(s, (8, 128))
        sst[0] = s if k == 0 else sst[0] + s

    pre(0)
    pl.semaphore_wait(barrier, len(peers))

    halves = (pl.ds(0, FH), pl.ds(FH, FH))

    def bunit(k):
        return h * 4 + (x + k) % 4

    def aunit(k):
        return (y + k) % 4

    lbs = {}

    def ag_sends(k):
        pa, pb = a_piece(y, k), b_piece(h * 4 + x, k)
        w = us(ROWS, FH)
        out = []
        for hr, hl in ((0, 1), (1, 0)):
            for ax, rd, ref, rows in (("y", yd, a_ref, pa), ("x", xd, b_ref, pb)):
                out.append((f"{ax}R{hr}{k}", ax + "+", w, lambda hh=hr, rd=rd, ref=ref, rows=rows: (
                    a_ref.at[pa, halves[hh]], ref.at[rows, halves[hh]], rd[1])))
                out.append((f"{ax}L{hl}{k}", ax + "-", w, lambda hh=hl, rd=rd, ref=ref, rows=rows: (
                    a_ref.at[pa, halves[hh]], ref.at[rows, halves[hh]], rd[3])))
        out.append((f"c0{k}", "c", ROWS * KB * 2 * CORE_US, lambda: (a_ref.at[pa, :], b_ref.at[pb, :], partner)))
        return out

    def local_b(k):
        c = pltpu.make_async_copy(a_ref.at[a_piece(y, k), :], b_ref.at[b_piece(h * 4 + x, k), :], lsem.at[12 + k])
        c.start()
        lbs[k] = c

    def cp(ref, rows, hh, device):
        return lambda: (ref.at[rows, hh], ref.at[rows, hh], device)

    add("ag0", 0.1, 0, lambda: local_b(0), sends=ag_sends(0))
    for k in (1, 3, 2):
        add(f"pre{k}", 0.6, 1, lambda k=k: pre(k), sends=[
            (f"z{k}", AXIS[k].format("z"), us(ROWS, KB), lambda k=k: (dbuf.at[k], a_ref.at[a_piece(y, 0), :], zd[k], zsem.at[z]))])

    def ag_start(j):
        c = pltpu.make_async_remote_copy(
            src_ref=dbuf.at[1], dst_ref=a_ref.at[a_piece(y, j), :], send_sem=send.at[0], recv_sem=zsem.at[slot(j)],
            device_id=zd[1], device_id_type=MESH)
        c.wait_recv()
        local_b(j)

    for j, src in ((1, ("z1", "z3")), (2, ("z2",)), (3, ("z2",))):
        add(f"ag{j}", 0.1, 0, lambda j=j: ag_start(j), after=src, sends=ag_sends(j),
            deps=[f"{ax}f{s}{j - 2}" for ax in "xy" for s in "RL"] if j >= 2 else [])
    for k in range(4):
        w = us(ROWS, FH)
        for ax, rd, ref, un, piece in (("y", yd, a_ref, aunit, a_piece), ("x", xd, b_ref, bunit, b_piece)):
            add(f"{ax}fR{k}", 0.05, 0, waits=[f"{ax}R0{k}"], sends=[
                (f"{ax}FR{k}", ax + "+", w, lambda k=k, rd=rd, ref=ref, un=un, piece=piece: cp(
                    ref, piece(un(3), k), halves[0], rd[1])())])
            add(f"{ax}fL{k}", 0.05, 0, waits=[f"{ax}L1{k}"], sends=[
                (f"{ax}FL{k}", ax + "-", w, lambda k=k, rd=rd, ref=ref, un=un, piece=piece: cp(
                    ref, piece(un(1), k), halves[1], rd[3])())])
        for j, ws, ds in ((3, [f"xR1{k}"], [f"xfR{k}"]), (1, [f"xL0{k}"], [f"xfL{k}"]), (2, [f"xFR{k}", f"xFL{k}"], [])):
            add(f"core{j}{k}", 0.05, 1, waits=ws, deps=ds, sends=[
                (f"c{j}{k}", "c", ROWS * KB * 2 * CORE_US,
                 lambda j=j, k=k: cp(b_ref, b_piece(bunit(j), k), pl.ds(0, KB), partner)())])

    stages = [("c", [partner]), ("z", [zd[1], zd[3], zd[2]]), ("y", [yd[1], yd[3], yd[2]]), ("x", [xd[1], xd[3], xd[2]])]

    def ss_sends(st):
        ax, devices = stages[st]
        return [(f"ss{st}{i}", ax if ax == "c" else AXIS[(1, 3, 2)[i]].format(ax), 0.01, lambda st=st, i=i, d=d: (sst.at[st], ssb.at[st, i], d)) for i, d in enumerate(devices)]

    def ss_add(st):
        tot = sst[st]
        for i in range(len(stages[st][1])):
            tot = tot + ssb[st, i]
        sst[st + 1] = tot

    add("ss0", 0.1, 2, deps=["pre1", "pre2", "pre3"], sends=ss_sends(0))
    for st in range(4):
        add(f"ss{st + 1}", 0.1, 2, lambda st=st: ss_add(st), waits=[f"ss{st}{i}" for i in range(len(stages[st][1]))],
            sends=ss_sends(st + 1) if st < 3 else [])

    def gathered(name, ks):
        def fn():
            for k in ks:
                lbs[k].wait()

        add(name, 0.1, 1, fn, deps=[f"ag{k}" for k in ks] + [f"{ax}f{s}{k}" for ax in "xy" for s in "RL" for k in ks]
            + [f"core{j}{k}" for j in (1, 2, 3) for k in ks],
            waits=[f"y{n}{k}" for n in ("R1", "L0", "FR", "FL") for k in ks] + [f"c{j}{k}" for j in range(4) for k in ks])

    gathered("agd1", (0, 1, 2))
    gathered("agd", (3,))

    def factor():
        return rms_target * math.sqrt(M) / (jnp.sqrt(sst[4][0:1, 0:1]) + 1e-07)

    def ring(tag, ax, pos, rd, part, r1, r2, full, w, prios, compute, comp_cost, comp_deps, add_cost, finish, comp_waits=(),
             sum_deps=(), sum_sends=()):
        def q(k):
            return (pos + k) % 4

        up, down = ax + "+", ax + "-"
        add(tag + "0", comp_cost, prios[0], compute, deps=comp_deps, waits=comp_waits, sends=[
            (tag + "A", up, w[0], lambda: (part(q(2), 0), r1(0), rd[1])),
            (tag + "B", down, w[1], lambda: (part(q(2), 1), r1(1), rd[3])),
            (tag + "C", up, w[1], lambda: (part(q(1), 1), r2(0, 1), rd[1])),
            (tag + "D", down, w[0], lambda: (part(q(3), 0), r2(1, 0), rd[3]))])

        def accumulate(k, hh):
            ref = part(q(k), hh)
            ref[...] = (ref[...].astype(F32) + r1(hh)[...].astype(F32)).astype(BF)

        add(tag + "1a", add_cost, prios[1], lambda: accumulate(1, 0), waits=[tag + "A"], sends=[
            (tag + "E", up, w[0], lambda: (part(q(1), 0), r2(0, 0), rd[1]))])
        add(tag + "1b", add_cost, prios[1], lambda: accumulate(3, 1), waits=[tag + "B"], sends=[
            (tag + "F", down, w[1], lambda: (part(q(3), 1), r2(1, 1), rd[3]))])

        def total():
            for hh in (0, 1):
                finish(hh, part(pos, hh)[...].astype(F32) + r2(0, hh)[...].astype(F32) + r2(1, hh)[...].astype(F32))

        sums = [tag + c for c in "CDEF"]
        if full is None:
            return total, sums
        add(tag + "2", 3 * add_cost, prios[2], total, waits=sums, sends=[
            (tag + "G", up, w[0], lambda: (full(pos, 0), full(pos, 0), rd[1])),
            (tag + "H", down, w[1], lambda: (full(pos, 1), full(pos, 1), rd[3])),
            (tag + "I", up, w[1], lambda: (full(pos, 1), full(pos, 1), rd[1])),
            (tag + "J", down, w[0], lambda: (full(pos, 0), full(pos, 0), rd[3]))] + list(sum_sends), deps=list(sum_deps))
        add(tag + "3a", 0.05, prios[3], waits=[tag + "G"], sends=[
            (tag + "K", up, w[0], lambda: (full(q(3), 0), full(q(3), 0), rd[1]))])
        add(tag + "3b", 0.05, prios[3], waits=[tag + "H"], sends=[
            (tag + "L", down, w[1], lambda: (full(q(1), 1), full(q(1), 1), rd[3]))])
        return [tag + c for c in "IJKL"], [tag + "3a", tag + "3b"]

    g_waits = {}
    g_deps = {}
    for b, (t, c) in enumerate(G_SEQ):
        rows, gcols = pl.ds(t * TR, TR), pl.ds(C_0[c], C_W[c])
        half = C_W[c] // 2

        def g_mm(rows=rows, gcols=gcols):
            gp[rows, gcols] = lax.dot_general(
                a_ref[rows, :], b_ref[gcols, :], (((1,), (1,)), ((), ())), preferred_element_type=F32).astype(BF)

        def g_part(buf, t=t, c=c, half=half):
            return lambda q, hh: buf.at[pl.ds(al(t * TR + q * QR), QR), pl.ds(C_0[c] + hh * half, half)]

        def g_finish(hh, tot, full=g_part(gf)):
            f = factor()
            full(z, hh)[...] = (tot * jnp.broadcast_to(f * f, tot.shape)).astype(BF)

        prev = [f"g{G_SEQ[b - WINDOW_G][0]}{G_SEQ[b - WINDOW_G][1]}2"] if b >= WINDOW_G else []
        g_waits[t, c], g_deps[t, c] = ring(
            f"g{t}{c}", "z", z, zd, g_part(gp),
            lambda hh, b=b, half=half: g1buf.at[b, hh, :, pl.ds(0, half)],
            lambda s, hh, b=b, half=half: g2buf.at[b, s, hh, :, pl.ds(0, half)],
            g_part(gf), [us(QR, half)] * 2, (30 + b, 2 + b, 2 + b, 2 + b), g_mm, 9.2 * C_W[c] / BR / T,
            ["agd1", "agd"][: 1 if t < 2 and c == 0 else 2] + prev, 0.05, g_finish, sum_deps=["ss4"])

    def g_ready(t, c):
        name = f"gd{t}{c}"

        def transpose(t=t, c=c):
            rows, gcols = pl.ds(t * TR, TR), pl.ds(C_0[c], C_W[c])
            gt[t, gcols, :] = gf[rows, gcols].T

        add(name, 0.1, 12, transpose, waits=g_waits[t, c], deps=g_deps[t, c])
        return name

    ready = {(t, c): g_ready(t, c) for t, c in G_SEQ}

    f_waits = []
    f_deps = []
    for t in range(T):
        rows = pl.ds(t * TR, TR)

        def f_mm(rows=rows):
            def body(j, carry):
                js = pl.ds(al(j * 512, 512), 512)
                fp[rows, js] = jnp.dot(gf[rows, :], b_ref[:, js], preferred_element_type=F32).astype(BF)
                return carry

            lax.fori_loop(0, N1 // 512, body, 0)

        def f_part(buf, t=t):
            return lambda q, hh: buf.at[pl.ds(al(t * TR + q * QR), QR), pl.ds(hh * F1H, F1H)]

        def f_finish(hh, tot, t=t, full=f_part(hf)):
            d = a_ref[pl.ds(al(t * TR + y * QR), QR), pl.ds(hh * F1H, F1H)].astype(F32)
            full(y, hh)[...] = (coef_b * d + coef_c * tot).astype(BF)

        fw, fd = ring(
            f"f{t}", "y", y, yd, f_part(fp), lambda hh, t=t: f1buf.at[t, hh], lambda s, hh, t=t: f2buf.at[t, s, hh],
            f_part(hf), [us(QR, F1H)] * 2, (15 + t, 1 + t, 1 + t, 1 + t), f_mm, 3.8 / T,
            [ready[t, c] for c in range(CT)] + ([f"f{t - WINDOW_F}2"] if t >= WINDOW_F else []), 0.05, f_finish)
        f_waits += fw
        f_deps += fd

    p_waits = []
    p_deps = []
    p_names = []
    for c in range(CT):
        core_rows = C_W[c] // 2
        q2 = core_rows // RING
        for j in range(P2):
            js = pl.ds(j * W2, W2)

            def p_rows(hb, c=c, core_rows=core_rows):
                return pl.ds(al(C_0[c] + hb * core_rows), core_rows)

            def p_mm(hb, c=c, j=j, p_rows=p_rows, core_rows=core_rows):
                acc = jnp.zeros((core_rows, W2), F32)
                for t in range(T):
                    acc = acc + jnp.dot(gt[t, p_rows(hb), :], a_ref[pl.ds(t * TR, TR), pl.ds(N1 + j * W2, W2)],
                                        preferred_element_type=F32)
                pp[p_rows(hb), pl.ds(j * W2, W2)] = acc.astype(BF)

            tag = f"p{c}{j}"
            i = len(p_names)
            p_names.append(tag)
            prev = [f"{p_names[i - WINDOW_P]}2"] if i >= WINDOW_P else []
            add(tag + "x", 1.85 * C_W[c] / BR / P2, 20 + i, lambda p_mm=p_mm: p_mm(1 - h), deps=[ready[t, c] for t in range(T)] + prev, sends=[
                (tag + "X", "c", core_rows * W2 * 2 * CORE_US, lambda p_rows=p_rows, js=js, c=c, core_rows=core_rows: (
                    pp.at[p_rows(1 - h), js], pr.at[pl.ds(C_0[c] // 2, core_rows), js], partner))])
            add(tag + "y", 1.85 * C_W[c] / BR / P2, 19 + i, lambda p_mm=p_mm: p_mm(h), deps=[tag + "x"])

            def p_add(p_rows=p_rows, js=js, c=c, core_rows=core_rows):
                r = p_rows(h)
                pp[r, js] = (pp[r, js].astype(F32) + pr[pl.ds(C_0[c] // 2, core_rows), js].astype(F32)).astype(BF)

            def p_part(buf, c=c, j=j, core_rows=core_rows, q2=q2):
                return lambda q, hh: buf.at[pl.ds(al(C_0[c] + h * core_rows + q * q2), q2), pl.ds(j * W2 + hh * (W2 // 2), W2 // 2)]

            def p_quarter(k, c=c, js=js, core_rows=core_rows, q2=q2):
                ref = hp.at[pl.ds(al(C_0[c] + h * core_rows + (x + k) % 4 * q2), q2), js]
                return ref, ref, partner

            def p_finish(hh, tot, c=c, j=j, core_rows=core_rows, q2=q2, full=p_part(hp)):
                d = b_ref[pl.ds(al(C_0[c] + h * core_rows + x * q2), q2), pl.ds(N1 + j * W2 + hh * (W2 // 2), W2 // 2)].astype(F32)
                full(x, hh)[...] = (coef_b * d + coef_c * tot).astype(BF)

            core_us = q2 * W2 * 2 * CORE_US
            pw, pd = ring(
                tag, "x", x, xd, p_part(pp), lambda hh, c=c, j=j, q2=q2: p1buf.at[c, j, hh, pl.ds(0, q2)],
                lambda s, hh, c=c, j=j, q2=q2: p2buf.at[c, j, s, hh, pl.ds(0, q2)],
                p_part(hp), [us(q2, W2 // 2)] * 2, (3 + i, 1, 1, 1), p_add, 0.1, [tag + "y"], 0.05, p_finish,
                comp_waits=[tag + "X"], sum_sends=[(tag + "q0", "c", core_us, lambda p_quarter=p_quarter: p_quarter(0))])
            for k, ws, ds in ((3, pw[0:1], pd[0:1]), (1, pw[1:2], pd[1:2]), (2, pw[2:], [])):
                add(f"{tag}c{k}", 0.05, 1, waits=ws, deps=ds, sends=[
                    (f"{tag}q{k}", "c", core_us, lambda p_quarter=p_quarter, k=k: p_quarter(k))])
            p_waits += [f"{tag}q{k}" for k in range(4)]
            p_deps += pd + [f"{tag}c{k}" for k in (1, 2, 3)]

    add("hd", 0.0, 0, deps=f_deps + [ready[k] for k in ready], waits=f_waits)
    add("hpd", 0.0, 0, deps=p_deps + [ready[k] for k in ready], waits=p_waits)

    own_out = []

    def send_back(tag, n, total, sums):
        ns = pl.ds(n * NW, NW)
        oc = pl.ds(al(z * KB + n * NW, 128), NW)

        def fin():
            total()
            c = pltpu.make_async_copy(ub.at[pl.ds(al(z * ROWS), ROWS), ns], out_ref.at[:, oc], lsem.at[16 + n])
            c.start()
            own_out.append(c)

        add(tag + "2", 0.1, 0, fin, waits=sums, sends=[
            (f"o{n}{k}", AXIS[k].format("z"), us(ROWS, NW),
             lambda k=k: (ub.at[pl.ds(al(((z + k) % 4) * ROWS), ROWS), ns], out_ref.at[:, oc], zd[k]))
            for k in (2, 1, 3)])

    for n in range(NT):
        ns = pl.ds(n * NW, NW)
        tag = f"s{n}"

        def s_finish(hh, tot, ns=ns):
            d = jnp.concatenate([a_ref[pl.ds(al(p * UNIT + y * ROWS), ROWS), ns].astype(F32) for p in (2 * hh, 2 * hh + 1)], axis=0)
            u = (coef_a * d + tot) * jnp.broadcast_to(factor() * scale_out, tot.shape)
            ub[pl.ds(hh * UH, UH), ns] = u.astype(BF)

        bufs = (lambda hh, n=n: s1buf.at[n, hh], lambda s, hh, n=n: s2buf.at[n, s, hh])
        if n < S1:
            def s_mm(hb, n=n, ns=ns):
                for p in range(RING):
                    r = pl.ds(al(p * 2 * UNIT + hb * UNIT), UNIT)
                    acc = jnp.zeros((UNIT, NW), F32)
                    for t in range(T):
                        acc = acc + jnp.dot(gt[t, r, :], hf[pl.ds(t * TR, TR), ns], preferred_element_type=F32)
                    tot = acc.astype(BF)
                    for i in range(RING):
                        sp[n, hb, i, p * ROWS:(p + 1) * ROWS, :] = tot[i * ROWS:(i + 1) * ROWS, :]

            def s_add(n=n):
                for i in range(RING):
                    sp[n, h, i] = (sp[n, h, i].astype(F32) + sr[n, i].astype(F32)).astype(BF)

            prev = [f"s{n - WINDOW_S}1a"] if n >= WINDOW_S else []
            add(tag + "x", 0.46, 40 + n, lambda s_mm=s_mm: s_mm(1 - h), deps=["hd"] + prev, sends=[
                (tag + "X", "c", AR * NW * 2 * CORE_US, lambda n=n: (sp.at[n, 1 - h], sr.at[n], partner))])
            add(tag + "y", 0.46, 39 + n, lambda s_mm=s_mm: s_mm(h), deps=[tag + "x"])
            total, sums = ring(
                tag, "x", x, xd, lambda q, hh, n=n: sp.at[n, h, q, pl.ds(hh * UH, UH), :], *bufs, None,
                [us(UH, NW)] * 2, (7, 1, 1, 1), s_add, 0.15, [tag + "y"], 0.05, s_finish, comp_waits=[tag + "X"])
        else:
            m = n - S1

            def v_mm(m=m):
                tot = jnp.dot(gf[...], hp[:, pl.ds(m * NW, NW)], preferred_element_type=F32).astype(BF)
                for p in range(RING):
                    for i in range(RING):
                        r = p * UNIT + i * ROWS
                        vp[m, i, p * ROWS:(p + 1) * ROWS, :] = tot[r:r + ROWS, :]

            prev = [f"s{n - WINDOW_S}1a"] if m >= WINDOW_S else []
            total, sums = ring(
                tag, "y", y, yd, lambda q, hh, m=m: vp.at[m, q, pl.ds(hh * UH, UH), :], *bufs, None,
                [us(UH, NW)] * 2, (40 + m, 1, 1, 1), v_mm, 0.85, ["hpd"] + prev, 0.05, s_finish)
        send_back(tag, n, total, sums)

    sched = order_of(tasks)
    if SHOW:
        SHOW(sched)
    for k, _, _ in sched:
        for w in k.waits:
            copies[w].wait_recv()
            waited.add(w)
        if k.fn is not None:
            k.fn()
        for name, _, _, make in k.sends:
            issue(name, *make())

    for name, c in copies.items():
        if name not in waited:
            c.wait_recv()
    for c in own_out + stores:
        c.wait()
    for c in copies.values():
        c.wait_send()


def muon(grad, momentum):
    def v(*shape):
        return pltpu.VMEM(shape, BF)

    hbm = pl.BlockSpec(memory_space=pl.ANY)
    return pl.pallas_call(
        kernel,
        out_shape=(jax.ShapeDtypeStruct((ROWS, N), BF), jax.ShapeDtypeStruct((ROWS, N), F32)),
        in_specs=[hbm, hbm],
        out_specs=(hbm, hbm),
        scratch_shapes=[
            pltpu.VMEM((RING, ROWS, KB), F32), pltpu.VMEM((RING, ROWS, KB), F32), v(RING, ROWS, KB),
            v(AR, KB), v(BR, KB),
            v(AR, BR), v(T * CT, 2, QR, CW_MAX // 2), v(T * CT, 2, 2, QR, CW_MAX // 2), v(AR, BR), v(T, BR, TR),
            v(AR, N1), v(T, 2, QR, F1H), v(T, 2, 2, QR, F1H), v(AR, N1),
            v(BR, N2), v(BR // 2, N2), v(CT, P2, 2, CW_MAX // 8, W2 // 2), v(CT, P2, 2, 2, CW_MAX // 8, W2 // 2), v(BR, N2),
            v(S1, 2, RING, UNIT, NW), v(S1, RING, UNIT, NW), v(NT - S1, RING, UNIT, NW), v(NT, 2, UH, NW), v(NT, 2, 2, UH, NW),
            v(UNIT, KB),
            pltpu.VMEM((4, 3, 8, 128), F32), pltpu.VMEM((5, 8, 128), F32),
            pltpu.SemaphoreType.DMA((N_SEM,)), pltpu.SemaphoreType.DMA((N_SEM,)), pltpu.SemaphoreType.DMA((16 + NT,)), pltpu.SemaphoreType.DMA((RING,)),
        ],
        compiler_params=pltpu.CompilerParams(collective_id=0, has_side_effects=True, vmem_limit_bytes=63 << 20),
    )(grad, momentum)


def solution(mesh):
    return jax.shard_map(
        muon,
        mesh=mesh,
        in_specs=(P(("row", "col"), None), P(("row", "col"), None)),
        out_specs=(P(("row", "col"), None), P(("row", "col"), None)),
        check_vma=False,
    )
```

```python
import math

import jax
import jax.numpy as jnp
from jax import lax
from jax.experimental import pallas as pl
from jax.experimental.pallas import tpu as pltpu
from jax.sharding import PartitionSpec as P

M = 7168
N = 8192

momentum_coef = 0.95
rms_target = 0.4
coef_a = 3.4445
coef_b = -4.775
coef_c = 2.0315
scale_out = 0.2 * math.sqrt(max(M, N))

BF = jnp.bfloat16
F32 = jnp.float32
MESH = pl.DeviceIdType.MESH

RING = 4
ROWS = 56
UNIT = RING * ROWS
KB = N // RING
AR = RING * UNIT
BR = 2 * AR
T = 4
TR = AR // T
QR = TR // RING
C_W = (768, 768, 256)
C_0 = (0, 768, 1536)
CT = len(C_W)
CW_MAX = max(C_W)
G_SEQ = ((0, 0), (1, 0), (2, 0), (3, 0), (0, 1), (0, 2), (1, 1), (1, 2), (2, 1), (3, 1), (2, 2), (3, 2))
FH = KB // 2
N1 = 1024
N2 = KB - N1
F1H = N1 // 2
W2 = 512
P2 = N2 // W2
NW = 256
NT = KB // NW
S1 = N1 // NW
UH = UNIT // 2
N_SEM = 480
WINDOW_G = 4
WINDOW_F = 4
WINDOW_P = 4
WINDOW_S = 4

LINK_US = 1e6 / 44.5e9
CORE_US = 1e6 / 500e9
HOP_US = 2.5
COST_SCALE = 1.5
COST_EACH = 0.1
SHOW = None
AXIS = {1: "{0}+", 3: "{0}-", 2: "{0}+ {0}-"}


class Task:
    def __init__(self, name, cost, prio, fn=None, waits=(), sends=(), deps=(), after=()):
        self.name, self.cost, self.prio, self.fn = name, cost, prio, fn
        self.waits, self.sends, self.deps, self.after = list(waits), list(sends), list(deps), list(after)


def order_of(tasks):
    now, free, arrive, done, order = 0.0, {}, {}, set(), []
    todo = list(tasks)
    while todo:
        best = None
        for i, k in enumerate(todo):
            if any(d not in done for d in k.deps) or any(w not in arrive for w in k.waits + k.after):
                continue
            ready = max([arrive[w] for w in k.waits + k.after], default=0.0)
            key = (max(ready, now), k.prio, i)
            if best is None or key < best[0]:
                best = (key, k)
        key, k = best
        todo.remove(k)
        now = key[0] + k.cost * COST_SCALE + COST_EACH
        for name, links, us, _ in k.sends:
            fin = now
            for link in links.split():
                free[link] = max(now, free.get(link, 0.0)) + us
                fin = max(fin, free[link])
            arrive[name] = fin + HOP_US
        done.add(k.name)
        order.append((k, key[0], now))
    return order


def kernel(grad_ref, mom_ref, out_ref, gin, minb, dbuf, a_ref, b_ref, gp, g1buf, g2buf, gf, gt, fp, f1buf, f2buf, hf,
           pp, pr, p1buf, p2buf, hp, sp, sr, vp, s1buf, s2buf, ub, ssb, sst, send, recv, lsem, zsem):
    row = lax.axis_index("row")
    col = lax.axis_index("col")
    x = row % 4
    h = col % 2
    y = (col // 2) % 4
    z = (col // 8) * 2 + row // 4

    def dev(dx=0, dy=0, dz=0, dh=0):
        nx, ny, nz, nh = (x + dx) % 4, (y + dy) % 4, (z + dz) % 4, (h + dh) % 2
        return {"row": (nz % 2) * 4 + nx, "col": (nz // 2) * 8 + ny * 2 + nh}

    zd = {k: dev(dz=k) for k in (1, 2, 3)}
    yd = {k: dev(dy=k) for k in (1, 2, 3)}
    xd = {k: dev(dx=k) for k in (1, 2, 3)}
    partner = dev(dh=1)

    def al(v, m=8):
        return pl.multiple_of(v, m)

    def cols(k):
        return pl.ds(al(((z + k) % 4) * KB, 128), KB)

    loads = {}
    for k in (0, 1, 3, 2):
        loads[k] = [pltpu.make_async_copy(grad_ref.at[:, cols(k)], gin.at[k], lsem.at[2 * k]),
                    pltpu.make_async_copy(mom_ref.at[:, cols(k)], minb.at[k], lsem.at[2 * k + 1])]
        for c in loads[k]:
            c.start()

    barrier = pltpu.get_barrier_semaphore()
    peers = [partner] + [r[k] for r in (zd, yd, xd) for k in (1, 2, 3)]
    for p in peers:
        pl.semaphore_signal(barrier, inc=1, device_id=p, device_id_type=MESH)

    copies = {}
    waited = set()

    def issue(name, src, dst, device, recv_sem=None):
        i = len(copies)
        if recv_sem is not None:
            waited.add(name)
        c = pltpu.make_async_remote_copy(
            src_ref=src, dst_ref=dst, send_sem=send.at[i], recv_sem=recv.at[i] if recv_sem is None else recv_sem,
            device_id=device, device_id_type=MESH)
        c.start()
        copies[name] = c

    tasks = []

    def add(*args, **kw):
        tasks.append(Task(*args, **kw))

    def us(rows, columns):
        return rows * columns * 2 * LINK_US

    def slot(j):
        return z if j == 0 else j - 1 + (j + 3 - z) // 4

    def a_piece(unit, j):
        return pl.ds(al(slot(j) * UNIT + unit * ROWS), ROWS)

    def b_piece(unit, j):
        return pl.ds(al(slot(j) * 2 * UNIT + unit * ROWS), ROWS)

    def pre(k):
        for c in loads[k]:
            c.wait()
        g = gin[k]
        nm = momentum_coef * minb[k] + g
        d = g + momentum_coef * nm
        if k == 0:
            a_ref[a_piece(y, 0), :] = d.astype(BF)
        else:
            dbuf[k] = d.astype(BF)
        s = jnp.sum(jnp.sum(d * d, axis=0, keepdims=True), axis=1, keepdims=True)
        s = jnp.broadcast_to(s, (8, 128))
        sst[0] = s if k == 0 else sst[0] + s

    pre(0)
    pl.semaphore_wait(barrier, len(peers))

    halves = (pl.ds(0, FH), pl.ds(FH, FH))

    def bunit(k):
        return h * 4 + (x + k) % 4

    def aunit(k):
        return (y + k) % 4

    lbs = {}

    def ag_sends(k):
        pa, pb = a_piece(y, k), b_piece(h * 4 + x, k)
        w = us(ROWS, FH)
        out = []
        for hr, hl in ((0, 1), (1, 0)):
            for ax, rd, ref, rows in (("y", yd, a_ref, pa), ("x", xd, b_ref, pb)):
                out.append((f"{ax}R{hr}{k}", ax + "+", w, lambda hh=hr, rd=rd, ref=ref, rows=rows: (
                    a_ref.at[pa, halves[hh]], ref.at[rows, halves[hh]], rd[1])))
                out.append((f"{ax}L{hl}{k}", ax + "-", w, lambda hh=hl, rd=rd, ref=ref, rows=rows: (
                    a_ref.at[pa, halves[hh]], ref.at[rows, halves[hh]], rd[3])))
        out.append((f"c0{k}", "c", ROWS * KB * 2 * CORE_US, lambda: (a_ref.at[pa, :], b_ref.at[pb, :], partner)))
        return out

    def local_b(k):
        c = pltpu.make_async_copy(a_ref.at[a_piece(y, k), :], b_ref.at[b_piece(h * 4 + x, k), :], lsem.at[12 + k])
        c.start()
        lbs[k] = c

    def cp(ref, rows, hh, device):
        return lambda: (ref.at[rows, hh], ref.at[rows, hh], device)

    add("ag0", 0.1, 0, lambda: local_b(0), sends=ag_sends(0))
    for k in (1, 3, 2):
        add(f"pre{k}", 0.6, 1, lambda k=k: pre(k), sends=[
            (f"z{k}", AXIS[k].format("z"), us(ROWS, KB), lambda k=k: (dbuf.at[k], a_ref.at[a_piece(y, 0), :], zd[k], zsem.at[z]))])

    def ag_start(j):
        c = pltpu.make_async_remote_copy(
            src_ref=dbuf.at[1], dst_ref=a_ref.at[a_piece(y, j), :], send_sem=send.at[0], recv_sem=zsem.at[slot(j)],
            device_id=zd[1], device_id_type=MESH)
        c.wait_recv()
        local_b(j)

    for j, src in ((1, ("z1", "z3")), (2, ("z2",)), (3, ("z2",))):
        add(f"ag{j}", 0.1, 0, lambda j=j: ag_start(j), after=src, sends=ag_sends(j),
            deps=[f"{ax}f{s}{j - 2}" for ax in "xy" for s in "RL"] if j >= 2 else [])
    for k in range(4):
        w = us(ROWS, FH)
        for ax, rd, ref, un, piece in (("y", yd, a_ref, aunit, a_piece), ("x", xd, b_ref, bunit, b_piece)):
            add(f"{ax}fR{k}", 0.05, 0, waits=[f"{ax}R0{k}"], sends=[
                (f"{ax}FR{k}", ax + "+", w, lambda k=k, rd=rd, ref=ref, un=un, piece=piece: cp(
                    ref, piece(un(3), k), halves[0], rd[1])())])
            add(f"{ax}fL{k}", 0.05, 0, waits=[f"{ax}L1{k}"], sends=[
                (f"{ax}FL{k}", ax + "-", w, lambda k=k, rd=rd, ref=ref, un=un, piece=piece: cp(
                    ref, piece(un(1), k), halves[1], rd[3])())])
        for j, ws, ds in ((3, [f"xR1{k}"], [f"xfR{k}"]), (1, [f"xL0{k}"], [f"xfL{k}"]), (2, [f"xFR{k}", f"xFL{k}"], [])):
            add(f"core{j}{k}", 0.05, 1, waits=ws, deps=ds, sends=[
                (f"c{j}{k}", "c", ROWS * KB * 2 * CORE_US,
                 lambda j=j, k=k: cp(b_ref, b_piece(bunit(j), k), pl.ds(0, KB), partner)())])

    stages = [("c", [partner]), ("z", [zd[1], zd[3], zd[2]]), ("y", [yd[1], yd[3], yd[2]]), ("x", [xd[1], xd[3], xd[2]])]

    def ss_sends(st):
        ax, devices = stages[st]
        return [(f"ss{st}{i}", ax if ax == "c" else AXIS[(1, 3, 2)[i]].format(ax), 0.01, lambda st=st, i=i, d=d: (sst.at[st], ssb.at[st, i], d)) for i, d in enumerate(devices)]

    def ss_add(st):
        tot = sst[st]
        for i in range(len(stages[st][1])):
            tot = tot + ssb[st, i]
        sst[st + 1] = tot

    add("ss0", 0.1, 2, deps=["pre1", "pre2", "pre3"], sends=ss_sends(0))
    for st in range(4):
        add(f"ss{st + 1}", 0.1, 2, lambda st=st: ss_add(st), waits=[f"ss{st}{i}" for i in range(len(stages[st][1]))],
            sends=ss_sends(st + 1) if st < 3 else [])

    def gathered(name, ks):
        def fn():
            for k in ks:
                lbs[k].wait()

        add(name, 0.1, 1, fn, deps=[f"ag{k}" for k in ks] + [f"{ax}f{s}{k}" for ax in "xy" for s in "RL" for k in ks]
            + [f"core{j}{k}" for j in (1, 2, 3) for k in ks],
            waits=[f"y{n}{k}" for n in ("R1", "L0", "FR", "FL") for k in ks] + [f"c{j}{k}" for j in range(4) for k in ks])

    gathered("agd1", (0, 1, 2))
    gathered("agd", (3,))

    def factor():
        return rms_target * math.sqrt(M) / (jnp.sqrt(sst[4][0:1, 0:1]) + 1e-07)

    def ring(tag, ax, pos, rd, part, r1, r2, full, w, prios, compute, comp_cost, comp_deps, add_cost, finish, comp_waits=(),
             sum_deps=(), sum_sends=()):
        def q(k):
            return (pos + k) % 4

        up, down = ax + "+", ax + "-"
        add(tag + "0", comp_cost, prios[0], compute, deps=comp_deps, waits=comp_waits, sends=[
            (tag + "A", up, w[0], lambda: (part(q(2), 0), r1(0), rd[1])),
            (tag + "B", down, w[1], lambda: (part(q(2), 1), r1(1), rd[3])),
            (tag + "C", up, w[1], lambda: (part(q(1), 1), r2(0, 1), rd[1])),
            (tag + "D", down, w[0], lambda: (part(q(3), 0), r2(1, 0), rd[3]))])

        def accumulate(k, hh):
            ref = part(q(k), hh)
            ref[...] = (ref[...].astype(F32) + r1(hh)[...].astype(F32)).astype(BF)

        add(tag + "1a", add_cost, prios[1], lambda: accumulate(1, 0), waits=[tag + "A"], sends=[
            (tag + "E", up, w[0], lambda: (part(q(1), 0), r2(0, 0), rd[1]))])
        add(tag + "1b", add_cost, prios[1], lambda: accumulate(3, 1), waits=[tag + "B"], sends=[
            (tag + "F", down, w[1], lambda: (part(q(3), 1), r2(1, 1), rd[3]))])

        def total():
            for hh in (0, 1):
                finish(hh, part(pos, hh)[...].astype(F32) + r2(0, hh)[...].astype(F32) + r2(1, hh)[...].astype(F32))

        sums = [tag + c for c in "CDEF"]
        if full is None:
            return total, sums
        add(tag + "2", 3 * add_cost, prios[2], total, waits=sums, sends=[
            (tag + "G", up, w[0], lambda: (full(pos, 0), full(pos, 0), rd[1])),
            (tag + "H", down, w[1], lambda: (full(pos, 1), full(pos, 1), rd[3])),
            (tag + "I", up, w[1], lambda: (full(pos, 1), full(pos, 1), rd[1])),
            (tag + "J", down, w[0], lambda: (full(pos, 0), full(pos, 0), rd[3]))] + list(sum_sends), deps=list(sum_deps))
        add(tag + "3a", 0.05, prios[3], waits=[tag + "G"], sends=[
            (tag + "K", up, w[0], lambda: (full(q(3), 0), full(q(3), 0), rd[1]))])
        add(tag + "3b", 0.05, prios[3], waits=[tag + "H"], sends=[
            (tag + "L", down, w[1], lambda: (full(q(1), 1), full(q(1), 1), rd[3]))])
        return [tag + c for c in "IJKL"], [tag + "3a", tag + "3b"]

    g_waits = {}
    g_deps = {}
    for b, (t, c) in enumerate(G_SEQ):
        rows, gcols = pl.ds(t * TR, TR), pl.ds(C_0[c], C_W[c])
        half = C_W[c] // 2

        def g_mm(rows=rows, gcols=gcols):
            gp[rows, gcols] = lax.dot_general(
                a_ref[rows, :], b_ref[gcols, :], (((1,), (1,)), ((), ())), preferred_element_type=F32).astype(BF)

        def g_part(buf, t=t, c=c, half=half):
            return lambda q, hh: buf.at[pl.ds(al(t * TR + q * QR), QR), pl.ds(C_0[c] + hh * half, half)]

        def g_finish(hh, tot, full=g_part(gf)):
            f = factor()
            full(z, hh)[...] = (tot * jnp.broadcast_to(f * f, tot.shape)).astype(BF)

        prev = [f"g{G_SEQ[b - WINDOW_G][0]}{G_SEQ[b - WINDOW_G][1]}2"] if b >= WINDOW_G else []
        g_waits[t, c], g_deps[t, c] = ring(
            f"g{t}{c}", "z", z, zd, g_part(gp),
            lambda hh, b=b, half=half: g1buf.at[b, hh, :, pl.ds(0, half)],
            lambda s, hh, b=b, half=half: g2buf.at[b, s, hh, :, pl.ds(0, half)],
            g_part(gf), [us(QR, half)] * 2, (30 + b, 2 + b, 2 + b, 2 + b), g_mm, 9.2 * C_W[c] / BR / T,
            ["agd1", "agd"][: 1 if t < 2 and c == 0 else 2] + prev, 0.05, g_finish, sum_deps=["ss4"])

    def g_ready(t, c):
        name = f"gd{t}{c}"

        def transpose(t=t, c=c):
            rows, gcols = pl.ds(t * TR, TR), pl.ds(C_0[c], C_W[c])
            gt[t, gcols, :] = gf[rows, gcols].T

        add(name, 0.1, 12, transpose, waits=g_waits[t, c], deps=g_deps[t, c])
        return name

    ready = {(t, c): g_ready(t, c) for t, c in G_SEQ}

    f_waits = []
    f_deps = []
    for t in range(T):
        rows = pl.ds(t * TR, TR)

        def f_mm(rows=rows):
            def body(j, carry):
                js = pl.ds(al(j * 512, 512), 512)
                fp[rows, js] = jnp.dot(gf[rows, :], b_ref[:, js], preferred_element_type=F32).astype(BF)
                return carry

            lax.fori_loop(0, N1 // 512, body, 0)

        def f_part(buf, t=t):
            return lambda q, hh: buf.at[pl.ds(al(t * TR + q * QR), QR), pl.ds(hh * F1H, F1H)]

        def f_finish(hh, tot, t=t, full=f_part(hf)):
            d = a_ref[pl.ds(al(t * TR + y * QR), QR), pl.ds(hh * F1H, F1H)].astype(F32)
            full(y, hh)[...] = (coef_b * d + coef_c * tot).astype(BF)

        fw, fd = ring(
            f"f{t}", "y", y, yd, f_part(fp), lambda hh, t=t: f1buf.at[t, hh], lambda s, hh, t=t: f2buf.at[t, s, hh],
            f_part(hf), [us(QR, F1H)] * 2, (15 + t, 1 + t, 1 + t, 1 + t), f_mm, 3.8 / T,
            [ready[t, c] for c in range(CT)] + ([f"f{t - WINDOW_F}2"] if t >= WINDOW_F else []), 0.05, f_finish)
        f_waits += fw
        f_deps += fd

    p_waits = []
    p_deps = []
    p_names = []
    for c in range(CT):
        core_rows = C_W[c] // 2
        q2 = core_rows // RING
        for j in range(P2):
            js = pl.ds(j * W2, W2)

            def p_rows(hb, c=c, core_rows=core_rows):
                return pl.ds(al(C_0[c] + hb * core_rows), core_rows)

            def p_mm(hb, c=c, j=j, p_rows=p_rows, core_rows=core_rows):
                acc = jnp.zeros((core_rows, W2), F32)
                for t in range(T):
                    acc = acc + jnp.dot(gt[t, p_rows(hb), :], a_ref[pl.ds(t * TR, TR), pl.ds(N1 + j * W2, W2)],
                                        preferred_element_type=F32)
                pp[p_rows(hb), pl.ds(j * W2, W2)] = acc.astype(BF)

            tag = f"p{c}{j}"
            i = len(p_names)
            p_names.append(tag)
            prev = [f"{p_names[i - WINDOW_P]}2"] if i >= WINDOW_P else []
            add(tag + "x", 1.85 * C_W[c] / BR / P2, 20 + i, lambda p_mm=p_mm: p_mm(1 - h), deps=[ready[t, c] for t in range(T)] + prev, sends=[
                (tag + "X", "c", core_rows * W2 * 2 * CORE_US, lambda p_rows=p_rows, js=js, c=c, core_rows=core_rows: (
                    pp.at[p_rows(1 - h), js], pr.at[pl.ds(C_0[c] // 2, core_rows), js], partner))])
            add(tag + "y", 1.85 * C_W[c] / BR / P2, 19 + i, lambda p_mm=p_mm: p_mm(h), deps=[tag + "x"])

            def p_add(p_rows=p_rows, js=js, c=c, core_rows=core_rows):
                r = p_rows(h)
                pp[r, js] = (pp[r, js].astype(F32) + pr[pl.ds(C_0[c] // 2, core_rows), js].astype(F32)).astype(BF)

            def p_part(buf, c=c, j=j, core_rows=core_rows, q2=q2):
                return lambda q, hh: buf.at[pl.ds(al(C_0[c] + h * core_rows + q * q2), q2), pl.ds(j * W2 + hh * (W2 // 2), W2 // 2)]

            def p_quarter(k, c=c, js=js, core_rows=core_rows, q2=q2):
                ref = hp.at[pl.ds(al(C_0[c] + h * core_rows + (x + k) % 4 * q2), q2), js]
                return ref, ref, partner

            def p_finish(hh, tot, c=c, j=j, core_rows=core_rows, q2=q2, full=p_part(hp)):
                d = b_ref[pl.ds(al(C_0[c] + h * core_rows + x * q2), q2), pl.ds(N1 + j * W2 + hh * (W2 // 2), W2 // 2)].astype(F32)
                full(x, hh)[...] = (coef_b * d + coef_c * tot).astype(BF)

            core_us = q2 * W2 * 2 * CORE_US
            pw, pd = ring(
                tag, "x", x, xd, p_part(pp), lambda hh, c=c, j=j, q2=q2: p1buf.at[c, j, hh, pl.ds(0, q2)],
                lambda s, hh, c=c, j=j, q2=q2: p2buf.at[c, j, s, hh, pl.ds(0, q2)],
                p_part(hp), [us(q2, W2 // 2)] * 2, (3 + i, 1, 1, 1), p_add, 0.1, [tag + "y"], 0.05, p_finish,
                comp_waits=[tag + "X"], sum_sends=[(tag + "q0", "c", core_us, lambda p_quarter=p_quarter: p_quarter(0))])
            for k, ws, ds in ((3, pw[0:1], pd[0:1]), (1, pw[1:2], pd[1:2]), (2, pw[2:], [])):
                add(f"{tag}c{k}", 0.05, 1, waits=ws, deps=ds, sends=[
                    (f"{tag}q{k}", "c", core_us, lambda p_quarter=p_quarter, k=k: p_quarter(k))])
            p_waits += [f"{tag}q{k}" for k in range(4)]
            p_deps += pd + [f"{tag}c{k}" for k in (1, 2, 3)]

    add("hd", 0.0, 0, deps=f_deps + [ready[k] for k in ready], waits=f_waits)
    add("hpd", 0.0, 0, deps=p_deps + [ready[k] for k in ready], waits=p_waits)

    own_out = []

    def send_back(tag, n, total, sums):
        ns = pl.ds(n * NW, NW)
        oc = pl.ds(al(z * KB + n * NW, 128), NW)

        def fin():
            total()
            c = pltpu.make_async_copy(ub.at[pl.ds(al(z * ROWS), ROWS), ns], out_ref.at[:, oc], lsem.at[16 + n])
            c.start()
            own_out.append(c)

        add(tag + "2", 0.1, 0, fin, waits=sums, sends=[
            (f"o{n}{k}", AXIS[k].format("z"), us(ROWS, NW),
             lambda k=k: (ub.at[pl.ds(al(((z + k) % 4) * ROWS), ROWS), ns], out_ref.at[:, oc], zd[k]))
            for k in (2, 1, 3)])

    for n in range(NT):
        ns = pl.ds(n * NW, NW)
        tag = f"s{n}"

        def s_finish(hh, tot, ns=ns):
            d = jnp.concatenate([a_ref[pl.ds(al(p * UNIT + y * ROWS), ROWS), ns].astype(F32) for p in (2 * hh, 2 * hh + 1)], axis=0)
            u = (coef_a * d + tot) * jnp.broadcast_to(factor() * scale_out, tot.shape)
            ub[pl.ds(hh * UH, UH), ns] = u.astype(BF)

        bufs = (lambda hh, n=n: s1buf.at[n, hh], lambda s, hh, n=n: s2buf.at[n, s, hh])
        if n < S1:
            def s_mm(hb, n=n, ns=ns):
                for p in range(RING):
                    r = pl.ds(al(p * 2 * UNIT + hb * UNIT), UNIT)
                    acc = jnp.zeros((UNIT, NW), F32)
                    for t in range(T):
                        acc = acc + jnp.dot(gt[t, r, :], hf[pl.ds(t * TR, TR), ns], preferred_element_type=F32)
                    tot = acc.astype(BF)
                    for i in range(RING):
                        sp[n, hb, i, p * ROWS:(p + 1) * ROWS, :] = tot[i * ROWS:(i + 1) * ROWS, :]

            def s_add(n=n):
                for i in range(RING):
                    sp[n, h, i] = (sp[n, h, i].astype(F32) + sr[n, i].astype(F32)).astype(BF)

            prev = [f"s{n - WINDOW_S}1a"] if n >= WINDOW_S else []
            add(tag + "x", 0.46, 40 + n, lambda s_mm=s_mm: s_mm(1 - h), deps=["hd"] + prev, sends=[
                (tag + "X", "c", AR * NW * 2 * CORE_US, lambda n=n: (sp.at[n, 1 - h], sr.at[n], partner))])
            add(tag + "y", 0.46, 39 + n, lambda s_mm=s_mm: s_mm(h), deps=[tag + "x"])
            total, sums = ring(
                tag, "x", x, xd, lambda q, hh, n=n: sp.at[n, h, q, pl.ds(hh * UH, UH), :], *bufs, None,
                [us(UH, NW)] * 2, (7, 1, 1, 1), s_add, 0.15, [tag + "y"], 0.05, s_finish, comp_waits=[tag + "X"])
        else:
            m = n - S1

            def v_mm(m=m):
                tot = jnp.dot(gf[...], hp[:, pl.ds(m * NW, NW)], preferred_element_type=F32).astype(BF)
                for p in range(RING):
                    for i in range(RING):
                        r = p * UNIT + i * ROWS
                        vp[m, i, p * ROWS:(p + 1) * ROWS, :] = tot[r:r + ROWS, :]

            prev = [f"s{n - WINDOW_S}1a"] if m >= WINDOW_S else []
            total, sums = ring(
                tag, "y", y, yd, lambda q, hh, m=m: vp.at[m, q, pl.ds(hh * UH, UH), :], *bufs, None,
                [us(UH, NW)] * 2, (40 + m, 1, 1, 1), v_mm, 0.85, ["hpd"] + prev, 0.05, s_finish)
        send_back(tag, n, total, sums)

    sched = order_of(tasks)
    if SHOW:
        SHOW(sched)
    for k, _, _ in sched:
        for w in k.waits:
            copies[w].wait_recv()
            waited.add(w)
        if k.fn is not None:
            k.fn()
        for name, _, _, make in k.sends:
            issue(name, *make())

    for name, c in copies.items():
        if name not in waited:
            c.wait_recv()
    for c in own_out:
        c.wait()
    for c in copies.values():
        c.wait_send()


def muon(grad, momentum):
    def v(*shape):
        return pltpu.VMEM(shape, BF)

    hbm = pl.BlockSpec(memory_space=pl.ANY)
    return pl.pallas_call(
        kernel,
        out_shape=jax.ShapeDtypeStruct((ROWS, N), BF),
        in_specs=[hbm, hbm],
        out_specs=hbm,
        scratch_shapes=[
            pltpu.VMEM((RING, ROWS, KB), F32), pltpu.VMEM((RING, ROWS, KB), F32), v(RING, ROWS, KB),
            v(AR, KB), v(BR, KB),
            v(AR, BR), v(T * CT, 2, QR, CW_MAX // 2), v(T * CT, 2, 2, QR, CW_MAX // 2), v(AR, BR), v(T, BR, TR),
            v(AR, N1), v(T, 2, QR, F1H), v(T, 2, 2, QR, F1H), v(AR, N1),
            v(BR, N2), v(BR // 2, N2), v(CT, P2, 2, CW_MAX // 8, W2 // 2), v(CT, P2, 2, 2, CW_MAX // 8, W2 // 2), v(BR, N2),
            v(S1, 2, RING, UNIT, NW), v(S1, RING, UNIT, NW), v(NT - S1, RING, UNIT, NW), v(NT, 2, UH, NW), v(NT, 2, 2, UH, NW),
            v(UNIT, KB),
            pltpu.VMEM((4, 3, 8, 128), F32), pltpu.VMEM((5, 8, 128), F32),
            pltpu.SemaphoreType.DMA((N_SEM,)), pltpu.SemaphoreType.DMA((N_SEM,)), pltpu.SemaphoreType.DMA((16 + NT,)), pltpu.SemaphoreType.DMA((RING,)),
        ],
        compiler_params=pltpu.CompilerParams(collective_id=0, has_side_effects=True, vmem_limit_bytes=63 << 20),
    )(grad, momentum)


def shards(grad, momentum):
    return muon(grad, momentum), momentum_coef * momentum + grad


def solution(mesh):
    return jax.shard_map(
        shards,
        mesh=mesh,
        in_specs=(P(("row", "col"), None), P(("row", "col"), None)),
        out_specs=(P(("row", "col"), None), P(("row", "col"), None)),
        check_vma=False,
    )
```
